256 devices in a mesh: row: 16 (over z, core), col: 16 (over y, x).
Axes of the slice: x: 4, y: 4, z: 8, core: 2. Of those that a mesh axis runs over, the one named last changes fastest.
Arguments:
- eigenvectors: float32 [8192, 2048], P('row', 'col'), may hold values from -6 to 6
- aligned_vectors: float32 [2, 8192, 256], P(None, 'row', 'col'), may hold values from -0.3 to 1, as said below
- straddle_vectors: float32 [2, 8192, 256], P(None, 'row', 'col'), may hold values from -0.3 to 1, as said below
Outputs:
- transformed: float32 [8192, 2048], P('row', 'col')
The draws below stay inside these ranges and needn't reach their ends.
Inputs may be any that keep to these rules, and one draw needn't show every extreme that they name: `aligned_vectors`: within each block of 512 rows, column i is 1 in the block's row i and 0 in the rows above it. `straddle_vectors`: within each straddling block of the steps, column i is 1 in the block's row i and 0 in the rows above it.
All inputs are finite; a program needn't handle non-finite values.
Results may differ from the reference program's by a relative error of at most 0.00027.
Values sent between devices are 32-bit elements; how exact they have to be, the bound alone decides.
A program may use at most 128 MiB of HBM per device.

```python
import jax
import jax.numpy as jnp
from jax import lax

NB = 256
SWEEPS = 2
ORDER = 8192
EIGVECS = 2048
N_ROW = 16


def householder_columns(key, local_rows):
    column_ids = jnp.arange(NB)
    noise = 0.05 * jax.random.truncated_normal(key, -6.0, 6.0, (SWEEPS, ORDER, NB), jnp.float32)
    on_diagonal = local_rows[:, None] == column_ids[None, :]
    above_diagonal = local_rows[:, None] < column_ids[None, :]
    values = jnp.where(on_diagonal, 1.0, jnp.where(above_diagonal, 0.0, noise))
    return values.astype(jnp.float32)


def draw_aligned_vectors(key, part):
    local_rows = jnp.arange(ORDER) % (2 * NB)
    return householder_columns(jax.random.fold_in(key, 11), local_rows)


def draw_straddle_vectors(key, part):
    global_rows = jnp.arange(ORDER)
    within = global_rows % (2 * NB)
    local_rows = jnp.where(within < NB, jnp.where(global_rows < NB, within, within + NB), within - NB)
    return householder_columns(jax.random.fold_in(key, 23), local_rows)


def block_scale(rng, extent, shards, low, high):
    level, own = 1.0, jax.random.fold_in(rng, 6)
    for axis_at, parts in shards:
        heights = jnp.exp(jax.random.uniform(jax.random.fold_in(own, axis_at), (parts,), jnp.float32, low / len(shards), high / len(shards)))
        level = level * jnp.repeat(heights, extent[axis_at] // parts).reshape([-1 if axis == axis_at else 1 for axis in range(len(extent))])
    return level


def normal_values(stream_key, extent, deviation, most, shards=(), held_as=jnp.bfloat16):
    entries = jax.random.normal(stream_key, extent, jnp.float32) * deviation
    if len(shards) > 0:
        entries = block_scale(stream_key, extent, shards, -0.22, 0.18) * entries
    return jnp.clip(entries, min=-most, max=most).astype(held_as)


def setup_inputs(seed: int = 0) -> dict:
    seeds = jax.random.split(jax.random.key(seed), 4)
    eigenvectors = normal_values(seeds[0], (ORDER, EIGVECS), 1.0, 6.0, ((0, 16), (1, 16)), jnp.float32)
    aligned_vectors = draw_aligned_vectors(jax.random.fold_in(seeds[3], 71), 0)
    straddle_vectors = draw_straddle_vectors(jax.random.fold_in(seeds[3], 71), 0)
    return dict(eigenvectors=eigenvectors, aligned_vectors=aligned_vectors, straddle_vectors=straddle_vectors)


def matmul(left_side, right_side):
    return jnp.dot(left_side, right_side, precision=lax.Precision.HIGHEST, preferred_element_type=jnp.float32)


def square_product(left_side, right_side):
    return jnp.matmul(left_side, right_side, precision=lax.Precision.HIGHEST)


def cross_product(left_side, right_side):
    return lax.dot_general(left_side, right_side, (((0,), (0,)), ((), ())), precision=lax.Precision.HIGHEST, preferred_element_type=jnp.float32)


def small_inverse(upper_form):
    order_now = upper_form.shape[-1]
    diagonal_now = jnp.diagonal(upper_form, axis1=-2, axis2=-1)
    nilpotent = jnp.triu(upper_form, 1) / diagonal_now[..., :, None]
    identity_matrix = jnp.eye(order_now, dtype=upper_form.dtype)
    result = identity_matrix - nilpotent
    powered = nilpotent
    for level in range((order_now - 1).bit_length() - 1):
        powered = square_product(powered, powered)
        result = square_product(result, identity_matrix + powered)
    return result / diagonal_now[..., None, :]


def upper_inverse(upper_form):
    order_now = upper_form.shape[-1]
    if order_now <= 32:
        return small_inverse(upper_form)
    halfway = order_now // 2
    upper_left = upper_inverse(upper_form[..., :halfway, :halfway])
    lower_right = upper_inverse(upper_form[..., halfway:, halfway:])
    top_right = -square_product(square_product(upper_left, upper_form[..., :halfway, halfway:]), lower_right)
    bottom_left = jnp.zeros_like(top_right)
    top_rows = jnp.concatenate([upper_left, top_right], axis=-1)
    bottom_rows = jnp.concatenate([bottom_left, lower_right], axis=-1)
    return jnp.concatenate([top_rows, bottom_rows], axis=-2)


def triangle_factor(gram_matrix):
    upper_form = jnp.triu(gram_matrix, 1) + jnp.diag(0.5 * jnp.diag(gram_matrix))
    return upper_inverse(upper_form)


def reflect(row_slab, vectors, factor):
    return row_slab - matmul(vectors, matmul(factor, cross_product(vectors, row_slab)))


def reference(eigenvectors, aligned_vectors, straddle_vectors):
    half_rows = NB
    block_span = 2 * NB
    current = eigenvectors
    for sweep_index in range(SWEEPS):
        aligned_now = aligned_vectors[sweep_index]
        straddle_now = straddle_vectors[sweep_index]
        for device_row in range(N_ROW - 1, -1, -1):
            block_start = device_row * block_span
            top_start = block_start + half_rows
            top_vectors = straddle_now[top_start:top_start + half_rows]
            top_slab = current[top_start:top_start + half_rows]
            gram_matrix = cross_product(top_vectors, top_vectors)
            partial_value = cross_product(top_vectors, top_slab)
            if device_row + 1 < N_ROW:
                bottom_start = block_start + block_span
                bottom_vectors = straddle_now[bottom_start:bottom_start + half_rows]
                bottom_slab = current[bottom_start:bottom_start + half_rows]
                gram_matrix = gram_matrix + cross_product(bottom_vectors, bottom_vectors)
                partial_value = partial_value + cross_product(bottom_vectors, bottom_slab)
            coeffs = matmul(triangle_factor(gram_matrix), partial_value)
            current = current.at[top_start:top_start + half_rows].set(top_slab - matmul(top_vectors, coeffs))
            if device_row + 1 < N_ROW:
                current = current.at[bottom_start:bottom_start + half_rows].set(bottom_slab - matmul(bottom_vectors, coeffs))
            block_vectors = aligned_now[block_start:block_start + block_span]
            block_factor = triangle_factor(cross_product(block_vectors, block_vectors))
            current = current.at[block_start:block_start + block_span].set(reflect(current[block_start:block_start + block_span], block_vectors, block_factor))
        first_vectors = straddle_now[:half_rows]
        first_factor = triangle_factor(cross_product(first_vectors, first_vectors))
        current = current.at[:half_rows].set(reflect(current[:half_rows], first_vectors, first_factor))
    return current
```

```python
import jax
import jax.numpy as jnp
from jax import lax
from jax.experimental import pallas as pl
from jax.experimental.pallas import tpu as pltpu
from jax.sharding import PartitionSpec as P

NB = 256
SPAN = 2 * NB
SIDE = 4
MESH = pl.DeviceIdType.MESH
HIGH = lax.Precision.HIGH


def mm(left, right):
    return lax.dot_general(
        left, right, (((1,), (0,)), ((), ())), precision=HIGH, preferred_element_type=jnp.float32
    )


def mmt(left, right):
    return lax.dot_general(
        left, right, (((1,), (1,)), ((), ())), precision=HIGH, preferred_element_type=jnp.float32
    )


def lower_inverses(grams):
    row = lax.broadcasted_iota(jnp.int32, (NB, NB), 0)
    col = lax.broadcasted_iota(jnp.int32, (NB, NB), 1)
    on_diagonal = row == col
    eye = jnp.where(on_diagonal, 1.0, 0.0)
    small = (row // 32 == col // 32) & (row > col)
    down = [0.5 * jnp.sum(jnp.where(on_diagonal, g, 0.0), axis=1, keepdims=True) for g in grams]
    across = [0.5 * jnp.sum(jnp.where(on_diagonal, g, 0.0), axis=0, keepdims=True) for g in grams]
    powers = [jnp.where(small, g, 0.0) / d for g, d in zip(grams, down)]
    result = [eye - n for n in powers]
    for _ in range(4):
        powers = [mm(n, n) for n in powers]
        result = [t + mm(t, n) for t, n in zip(result, powers)]
    result = [t / d for t, d in zip(result, across)]
    for size in (32, 64, 128):
        below = (row // (2 * size) == col // (2 * size)) & (row // size > col // size)
        left = [mm(t, jnp.where(below, g, 0.0)) for t, g in zip(result, grams)]
        result = [t - mm(half, t) for t, half in zip(result, left)]
    return result


def kernel(
    c_ref, a_ref, x_ref, o_ref,
    A, X, Ct, gram_a, gram_l, gram_u, gram_in, t_a, t_l, t_u, g_t, h_t, b_1, b_2, m_t,
    p_own, p_in, P_own, P_in,
    ring_send, ring_recv, row_send, row_recv,
):
    row = lax.axis_index("row")
    col = lax.axis_index("col")
    last = lax.axis_size("row") - 1
    y, x = col // SIDE, col % SIDE

    def at_x(step):
        return (row, y * SIDE + (x + step + SIDE) % SIDE)

    def at_y(step):
        return (row, ((y + step + SIDE) % SIDE) * SIDE + x)

    above = ((row + last) % (last + 1), col)
    below = ((row + 1) % (last + 1), col)
    has_above = row > 0
    has_below = row < last

    def remote(src, dst, sems, index, device):
        send, recv = sems
        return pltpu.make_async_remote_copy(
            src_ref=src, dst_ref=dst, send_sem=send.at[index], recv_sem=recv.at[index],
            device_id=device, device_id_type=MESH,
        )

    ring = (ring_send, ring_recv)
    rows = (row_send, row_recv)

    barrier = pltpu.get_barrier_semaphore()
    for device in (at_x(1), at_x(-1), at_y(1), at_y(-1)):
        pl.semaphore_signal(barrier, inc=1, device_id=device, device_id_type=MESH)

    @pl.when(has_above)
    def _():
        pl.semaphore_signal(barrier, inc=1, device_id=above, device_id_type=MESH)

    @pl.when(has_below)
    def _():
        pl.semaphore_signal(barrier, inc=1, device_id=below, device_id_type=MESH)

    ends = (row + last) // (last + 1) + (2 * last - row) // (last + 1)
    pl.semaphore_wait(barrier, 4 + ends)

    def a_one(k):
        return A.at[:, y, (x + k + SIDE) % SIDE]

    def a_line(k):
        return A.at[:, (y + k + SIDE) % SIDE]

    def x_one(k):
        return X.at[:, (y + k + SIDE) % SIDE, x]

    def x_line(k):
        return X.at[:, :, (x + k + SIDE) % SIDE]

    def ring_stage(base, own, slot, device):
        right = remote(own, slot(0), ring, base, device(1))
        left = remote(own, slot(0), ring, base + 1, device(-1))
        on_right = remote(slot(-1).at[0], slot(-1).at[0], ring, base + 2, device(1))
        on_left = remote(slot(1).at[1], slot(1).at[1], ring, base + 3, device(-1))
        return right, left, on_right, on_left

    def begin(stage):
        stage[0].start()
        stage[1].start()

    def pass_on(stage):
        stage[0].wait_recv()
        stage[2].start()
        stage[1].wait_recv()
        stage[3].start()

    def finish(stage):
        stage[2].wait_recv()
        stage[3].wait_recv()

    stage_a1 = ring_stage(0, a_ref, a_one, at_x)
    stage_x1 = ring_stage(4, x_ref, x_one, at_y)
    stage_a2 = ring_stage(8, a_line(0), a_line, at_y)
    stage_x2 = ring_stage(12, x_line(0), x_line, at_x)

    begin(stage_x1)
    begin(stage_a1)
    A[:, y, x] = a_ref[...]
    X[:, y, x] = x_ref[...]

    @pl.when(row == last)
    def _():
        gram_in[...] = jnp.zeros_like(gram_in)
        P_in[...] = jnp.zeros_like(P_in)

    @pl.when(row == 0)
    def _():
        p_in[...] = jnp.zeros_like(p_in)

    pass_on(stage_x1)
    pass_on(stage_a1)
    finish(stage_x1)
    begin(stage_x2)
    finish(stage_a1)
    begin(stage_a2)
    Ct[...] = c_ref[...].T
    pass_on(stage_x2)
    pass_on(stage_a2)
    finish(stage_x2)

    def x_up(s):
        return X[s, :, :, :, :NB].reshape(NB, NB)

    def x_low(s):
        return X[s, :, :, :, NB:].reshape(NB, NB)

    def a_up(s):
        return A[s, :, :, :, :NB].reshape(NB, NB)

    def a_low(s):
        return A[s, :, :, :, NB:].reshape(NB, NB)

    def a_all(s):
        return A[s].reshape(NB, SPAN)

    gram_up = [remote(gram_u.at[s], gram_in.at[s], rows, s, above) for s in range(2)]
    t_down = [remote(t_l.at[s], t_u.at[s], rows, 2 + s, below) for s in range(2)]
    p_down = [remote(p_own.at[s], p_in.at[s], rows, 4 + s, below) for s in range(2)]
    P_up = [remote(P_own.at[s], P_in.at[s], rows, 6 + s, above) for s in range(2)]

    for s in range(2):
        gram_u[s] = mmt(x_up(s), x_up(s))

        @pl.when(has_above)
        def _():
            gram_up[s].start()

        gram_l[s] = mmt(x_low(s), x_low(s))

    p_own[0] = mmt(Ct[:, NB:], x_low(0))

    @pl.when(has_below)
    def _():
        p_down[0].start()

    finish(stage_a2)
    for s in range(2):
        gram_a[s] = mmt(a_all(s), a_all(s))
        g_t[s] = mmt(x_low(s), a_low(s))
        h_t[s] = mmt(a_up(s), x_up(s))
    pair = lower_inverses([gram_a[0], gram_a[1]])
    for s in range(2):
        t_a[s] = pair[s]
        b_2[s] = mm(t_a[s], h_t[s])

    @pl.when(has_below)
    def _():
        for s in range(2):
            gram_up[s].wait_recv()

    pair = lower_inverses([gram_l[0] + gram_in[0], gram_l[1] + gram_in[1]])
    for s in range(2):
        t_l[s] = pair[s]

        @pl.when(has_below)
        def _():
            t_down[s].start()

    for s in range(2):
        b_1[s] = mm(t_l[s], g_t[s])
        m_t[s] = mm(b_1[s], b_2[s])

    @pl.when(row == 0)
    def _():
        own = lower_inverses([gram_u[0], gram_u[1]])
        for s in range(2):
            t_u[s] = own[s]

    for s in range(2):
        w = mmt(Ct[...], a_all(s))
        base = mmt(Ct[:, :NB], x_up(s)) - mm(w, b_2[s])

        @pl.when(has_below)
        def _():
            P_up[s].wait_recv()

        both = p_own[s] + P_in[s]
        P_own[s] = base + mm(both, m_t[s])

        @pl.when(has_above)
        def _():
            P_up[s].start()

        coeffs_a = mm(w - mm(both, b_1[s]), t_a[s])
        coeffs_l = mm(both, t_l[s])
        Ct[:, NB:] = Ct[:, NB:] - mm(coeffs_l, x_low(s)) - mm(coeffs_a, a_low(s))
        if s == 0:
            p_own[1] = mmt(Ct[:, NB:], x_low(1))

            @pl.when(has_below)
            def _():
                p_down[1].start()

        @pl.when(has_above)
        def _():
            p_down[s].wait_recv()
            if s == 0:
                for later in range(2):
                    t_down[later].wait_recv()

        coeffs_u = mm(p_in[s] + P_own[s], t_u[s])
        Ct[:, :NB] = Ct[:, :NB] - mm(coeffs_a, a_up(s)) - mm(coeffs_u, x_up(s))

    o_ref[...] = Ct[...].T

    for stage in (stage_a1, stage_x1, stage_a2, stage_x2):
        for copy in stage:
            copy.wait_send()

    @pl.when(has_above)
    def _():
        for copy in gram_up + P_up:
            copy.wait_send()

    @pl.when(has_below)
    def _():
        for copy in t_down + p_down:
            copy.wait_send()


def on_device(eigenvectors, aligned_vectors, straddle_vectors):
    columns = eigenvectors.shape[1]
    whole = pl.BlockSpec(memory_space=pltpu.VMEM)
    square = pltpu.VMEM((2, NB, NB), jnp.float32)
    gathered = pltpu.VMEM((2, SIDE, SIDE, 16, SPAN), jnp.float32)
    product = pltpu.VMEM((2, columns, NB), jnp.float32)
    return pl.pallas_call(
        kernel,
        out_shape=jax.ShapeDtypeStruct(eigenvectors.shape, jnp.float32),
        in_specs=[whole] * 3,
        out_specs=whole,
        scratch_shapes=[gathered, gathered, pltpu.VMEM((columns, SPAN), jnp.float32)]
        + [square] * 12
        + [product] * 4
        + [
            pltpu.SemaphoreType.DMA((16,)),
            pltpu.SemaphoreType.DMA((16,)),
            pltpu.SemaphoreType.DMA((8,)),
            pltpu.SemaphoreType.DMA((8,)),
        ],
        compiler_params=pltpu.CompilerParams(
            collective_id=0, has_side_effects=True, vmem_limit_bytes=48 * 1024 * 1024
        ),
    )(
        eigenvectors,
        jnp.swapaxes(aligned_vectors, 1, 2),
        jnp.swapaxes(straddle_vectors, 1, 2),
    )


def solution(mesh):
    placed = (P("row", "col"), P(None, "row", "col"), P(None, "row", "col"))
    return jax.shard_map(
        on_device, mesh=mesh, in_specs=placed, out_specs=P("row", "col"), check_vma=False
    )
```

```python
import jax
import jax.numpy as jnp
from jax import lax
from jax.experimental import pallas as pl
from jax.experimental.pallas import tpu as pltpu
from jax.sharding import PartitionSpec as P

NB = 256
SPAN = 2 * NB
SIDE = 4
PIECES = 4
PIECE = 32
MESH = pl.DeviceIdType.MESH
HIGH = lax.Precision.HIGH


def mm(left, right):
    return lax.dot_general(
        left, right, (((1,), (0,)), ((), ())), precision=HIGH, preferred_element_type=jnp.float32
    )


def mmt(left, right):
    return lax.dot_general(
        left, right, (((1,), (1,)), ((), ())), precision=HIGH, preferred_element_type=jnp.float32
    )


def lower_inverses(grams, between=()):
    between = list(between)

    def pause():
        if between:
            between.pop(0)()

    row = lax.broadcasted_iota(jnp.int32, (NB, NB), 0)
    col = lax.broadcasted_iota(jnp.int32, (NB, NB), 1)
    on_diagonal = row == col
    eye = jnp.where(on_diagonal, 1.0, 0.0)
    small = (row // 32 == col // 32) & (row > col)
    down = [0.5 * jnp.sum(jnp.where(on_diagonal, g, 0.0), axis=1, keepdims=True) for g in grams]
    across = [0.5 * jnp.sum(jnp.where(on_diagonal, g, 0.0), axis=0, keepdims=True) for g in grams]
    powers = [jnp.where(small, g, 0.0) / d for g, d in zip(grams, down)]
    result = [eye - n for n in powers]
    for _ in range(4):
        powers = [mm(n, n) for n in powers]
        result = [t + mm(t, n) for t, n in zip(result, powers)]
    pause()
    result = [t / d for t, d in zip(result, across)]
    for size in (32, 64, 128):
        below = (row // (2 * size) == col // (2 * size)) & (row // size > col // size)
        left = [mm(t, jnp.where(below, g, 0.0)) for t, g in zip(result, grams)]
        result = [t - mm(half, t) for t, half in zip(result, left)]
        pause()
    return result


def kernel(
    c_ref, a_ref, x_ref, o_ref,
    V, C_in, Ct, gram_a, gram_l, gram_u, gram_in, t_a, t_l, t_u, g_t, h_t, b_1, b_2, m_t,
    p_own, p_in, P_own, P_in,
    ring_send, ring_recv, row_send, row_recv, chain_send, chain_recv, local_sem,
):
    row = lax.axis_index("row")
    col = lax.axis_index("col")
    last = lax.axis_size("row") - 1
    y, x = col // SIDE, col % SIDE

    def at_x(step):
        return (row, y * SIDE + (x + step + SIDE) % SIDE)

    def at_y(step):
        return (row, ((y + step + SIDE) % SIDE) * SIDE + x)

    above = ((row + last) % (last + 1), col)
    below = ((row + 1) % (last + 1), col)
    has_above = row > 0
    has_below = row < last

    def remote(src, dst, sems, index, device):
        send, recv = sems
        return pltpu.make_async_remote_copy(
            src_ref=src, dst_ref=dst, send_sem=send.at[index], recv_sem=recv.at[index],
            device_id=device, device_id_type=MESH,
        )

    ring = (ring_send, ring_recv)
    rows = (row_send, row_recv)
    chain = (chain_send, chain_recv)

    barrier = pltpu.get_barrier_semaphore()
    for device in (at_x(1), at_x(-1), at_y(1), at_y(-1)):
        pl.semaphore_signal(barrier, inc=1, device_id=device, device_id_type=MESH)

    @pl.when(has_above)
    def _():
        pl.semaphore_signal(barrier, inc=1, device_id=above, device_id_type=MESH)

    @pl.when(has_below)
    def _():
        pl.semaphore_signal(barrier, inc=1, device_id=below, device_id_type=MESH)

    def own_block(group, half):
        source = x_ref if group % 2 == 0 else a_ref
        return source.at[group // 2, :, pl.ds((1 - half) * NB, NB)]

    def one(group, half, k):
        if half == 0:
            return V.at[group, half, y, (x + k + SIDE) % SIDE]
        return V.at[group, half, (y + k + SIDE) % SIDE, x]

    def line(group, half, k):
        if half == 0:
            return V.at[group, half, (y + k + SIDE) % SIDE]
        return V.at[group, half, :, (x + k + SIDE) % SIDE]

    own_copies = [
        pltpu.make_async_copy(own_block(g, h), one(g, h, 0), local_sem.at[2 * g + h])
        for g in range(4) for h in range(2)
    ]
    c_copy = pltpu.make_async_copy(c_ref, C_in, local_sem.at[8])
    for copy in own_copies:
        copy.start()
    c_copy.start()

    def ring_stage(base, own, slot, device, split):
        first, second = pl.ds(0, split), pl.ds(split, split)
        return (
            remote(own, slot(0), ring, base, device(1)),
            remote(own, slot(0), ring, base + 1, device(-1)),
            remote(slot(-1).at[first], slot(-1).at[first], ring, base + 2, device(1)),
            remote(slot(1).at[second], slot(1).at[second], ring, base + 3, device(-1)),
        )

    def begin(stage):
        stage[0].start()
        stage[1].start()

    def pass_on(stage):
        stage[0].wait_recv()
        stage[2].start()
        stage[1].wait_recv()
        stage[3].start()

    def finish(stage):
        stage[2].wait_recv()
        stage[3].wait_recv()

    near, far = {}, {}
    for g in range(4):
        for h in range(2):
            base = 8 * (2 * g + h)
            axes = (at_x, at_y) if h == 0 else (at_y, at_x)
            near[g, h] = ring_stage(
                base, own_block(g, h), lambda k, g=g, h=h: one(g, h, k), axes[0], 8
            )
            far[g, h] = ring_stage(
                base + 4, line(g, h, 0), lambda k, g=g, h=h: line(g, h, k), axes[1], 2
            )

    def near_to_far(g):
        for h in range(2):
            finish(near[g, h])
            begin(far[g, h])

    def far_pass(g):
        for h in range(2):
            pass_on(far[g, h])

    def far_finish(g):
        for h in range(2):
            finish(far[g, h])

    ends = (row + last) // (last + 1) + (2 * last - row) // (last + 1)
    pl.semaphore_wait(barrier, 4 + ends)
    for g in range(4):
        for h in range(2):
            begin(near[g, h])

    @pl.when(row == last)
    def _():
        gram_in[...] = jnp.zeros_like(gram_in)
        P_in[...] = jnp.zeros_like(P_in)

    @pl.when(row == 0)
    def _():
        p_in[...] = jnp.zeros_like(p_in)

    for copy in own_copies:
        copy.wait()
    for g in range(4):
        for h in range(2):
            pass_on(near[g, h])
    near_to_far(0)
    near_to_far(1)
    c_copy.wait()
    Ct[...] = C_in[...].T
    far_pass(0)
    near_to_far(2)
    far_pass(1)
    near_to_far(3)

    def x_up(s):
        return V[2 * s, 1].reshape(NB, NB)

    def x_low(s):
        return V[2 * s, 0].reshape(NB, NB)

    def a_up(s):
        return V[2 * s + 1, 1].reshape(NB, NB)

    def a_low(s):
        return V[2 * s + 1, 0].reshape(NB, NB)

    gram_up = [remote(gram_u.at[s], gram_in.at[s], rows, s, above) for s in range(2)]
    t_down = [remote(t_l.at[s], t_u.at[s], rows, 2 + s, below) for s in range(2)]
    p_down = [remote(p_own.at[s], p_in.at[s], rows, 4 + s, below) for s in range(2)]
    P_up = [
        [
            remote(
                P_own.at[s, pl.ds(k * PIECE, PIECE)], P_in.at[s, pl.ds(k * PIECE, PIECE)],
                chain, s * PIECES + k, above,
            )
            for k in range(PIECES)
        ]
        for s in range(2)
    ]

    def upper_gram(s):
        gram_u[s] = mmt(x_up(s), x_up(s))

        @pl.when(has_above)
        def _():
            gram_up[s].start()

    def aligned_products(s):
        gram_a[s] = mmt(a_up(s), a_up(s)) + mmt(a_low(s), a_low(s))

    def cross_products(s):
        g_t[s] = mmt(x_low(s), a_low(s))
        h_t[s] = mmt(a_up(s), x_up(s))

    far_finish(0)
    upper_gram(0)
    gram_l[0] = mmt(x_low(0), x_low(0))
    p_own[0] = mmt(Ct[:, NB:], x_low(0))

    @pl.when(has_below)
    def _():
        p_down[0].start()

    far_finish(1)
    aligned_products(0)
    far_pass(2)

    def third_ready():
        far_finish(2)
        upper_gram(1)

    def last_ready():
        far_pass(3)

    t_a[0] = lower_inverses([gram_a[0]], (last_ready, third_ready))[0]
    cross_products(0)
    b_2[0] = mm(t_a[0], h_t[0])
    gram_l[1] = mmt(x_low(1), x_low(1))
    far_finish(3)
    aligned_products(1)
    cross_products(1)

    @pl.when(has_below)
    def _():
        for s in range(2):
            gram_up[s].wait_recv()

    three = lower_inverses([gram_l[0] + gram_in[0], gram_l[1] + gram_in[1], gram_a[1]])
    for s in range(2):
        t_l[s] = three[s]

        @pl.when(has_below)
        def _():
            t_down[s].start()

    t_a[1] = three[2]
    b_2[1] = mm(t_a[1], h_t[1])
    for s in range(2):
        b_1[s] = mm(t_l[s], g_t[s])
        m_t[s] = mm(b_1[s], b_2[s])

    @pl.when(row == 0)
    def _():
        own = lower_inverses([gram_u[0], gram_u[1]])
        for s in range(2):
            t_u[s] = own[s]

    for s in range(2):
        upper, lower = Ct[:, :NB], Ct[:, NB:]
        w = mmt(upper, a_up(s)) + mmt(lower, a_low(s))
        P_own[s] = mmt(upper, x_up(s)) - mm(w, b_2[s]) + mm(p_own[s], m_t[s])
        for k in range(PIECES):
            piece = pl.ds(k * PIECE, PIECE)

            @pl.when(has_below)
            def _():
                P_up[s][k].wait_recv()
                P_own[s, piece] += mm(P_in[s, piece], m_t[s])

            @pl.when(has_above)
            def _():
                P_up[s][k].start()

        both = p_own[s] + P_in[s]
        coeffs_a = mm(w - mm(both, b_1[s]), t_a[s])
        coeffs_l = mm(both, t_l[s])
        Ct[:, NB:] = lower - mm(coeffs_l, x_low(s)) - mm(coeffs_a, a_low(s))
        if s == 0:
            p_own[1] = mmt(Ct[:, NB:], x_low(1))

            @pl.when(has_below)
            def _():
                p_down[1].start()

        @pl.when(has_above)
        def _():
            p_down[s].wait_recv()
            if s == 0:
                for later in range(2):
                    t_down[later].wait_recv()

        coeffs_u = mm(p_in[s] + P_own[s], t_u[s])
        Ct[:, :NB] = upper - mm(coeffs_a, a_up(s)) - mm(coeffs_u, x_up(s))

    o_ref[...] = Ct[...].T

    for stages in (near, far):
        for stage in stages.values():
            for copy in stage:
                copy.wait_send()

    @pl.when(has_above)
    def _():
        for copy in gram_up + P_up[0] + P_up[1]:
            copy.wait_send()

    @pl.when(has_below)
    def _():
        for copy in t_down + p_down:
            copy.wait_send()


def on_device(eigenvectors, aligned_vectors, straddle_vectors):
    columns = eigenvectors.shape[1]
    in_place = pl.BlockSpec(memory_space=pl.ANY)
    square = pltpu.VMEM((2, NB, NB), jnp.float32)
    product = pltpu.VMEM((2, columns, NB), jnp.float32)
    dma = pltpu.SemaphoreType.DMA
    return pl.pallas_call(
        kernel,
        out_shape=jax.ShapeDtypeStruct(eigenvectors.shape, jnp.float32),
        in_specs=[in_place] * 3,
        out_specs=pl.BlockSpec(memory_space=pltpu.VMEM),
        scratch_shapes=[
            pltpu.VMEM((4, 2, SIDE, SIDE, NB // SIDE**2, NB), jnp.float32),
            pltpu.VMEM(eigenvectors.shape, jnp.float32),
            pltpu.VMEM((columns, SPAN), jnp.float32),
        ]
        + [square] * 12
        + [product] * 4
        + [dma((64,)), dma((64,)), dma((6,)), dma((6,)), dma((2 * PIECES,)), dma((2 * PIECES,)), dma((9,))],
        compiler_params=pltpu.CompilerParams(
            collective_id=0, has_side_effects=True, vmem_limit_bytes=56 * 1024 * 1024
        ),
    )(
        eigenvectors,
        jnp.swapaxes(aligned_vectors, 1, 2),
        jnp.swapaxes(straddle_vectors, 1, 2),
    )


def solution(mesh):
    placed = (P("row", "col"), P(None, "row", "col"), P(None, "row", "col"))
    return jax.shard_map(
        on_device, mesh=mesh, in_specs=placed, out_specs=P("row", "col"), check_vma=False
    )
```

```python
import jax
import jax.numpy as jnp
from jax import lax
from jax.experimental import pallas as pl
from jax.experimental.pallas import tpu as pltpu
from jax.sharding import PartitionSpec as P

NB = 256
SPAN = 2 * NB
HALF = NB // 2
SIDE = 4
PIECES = 4
PIECE = 32
MESH = pl.DeviceIdType.MESH
HIGH = lax.Precision.HIGH


def mm(left, right):
    return lax.dot_general(
        left, right, (((1,), (0,)), ((), ())), precision=HIGH, preferred_element_type=jnp.float32
    )


def mmt(left, right):
    return lax.dot_general(
        left, right, (((1,), (1,)), ((), ())), precision=HIGH, preferred_element_type=jnp.float32
    )


def lower_inverses(grams, between=()):
    between = list(between)

    def pause():
        if between:
            between.pop(0)()

    row = lax.broadcasted_iota(jnp.int32, (NB, NB), 0)
    col = lax.broadcasted_iota(jnp.int32, (NB, NB), 1)
    on_diagonal = row == col
    eye = jnp.where(on_diagonal, 1.0, 0.0)
    small = (row // 32 == col // 32) & (row > col)
    down = [0.5 * jnp.sum(jnp.where(on_diagonal, g, 0.0), axis=1, keepdims=True) for g in grams]
    across = [0.5 * jnp.sum(jnp.where(on_diagonal, g, 0.0), axis=0, keepdims=True) for g in grams]
    powers = [jnp.where(small, g, 0.0) / d for g, d in zip(grams, down)]
    result = [eye - n for n in powers]
    for _ in range(4):
        powers = [mm(n, n) for n in powers]
        result = [t + mm(t, n) for t, n in zip(result, powers)]
    pause()
    result = [t / d for t, d in zip(result, across)]
    for size in (32, 64, 128):
        below = (row // (2 * size) == col // (2 * size)) & (row // size > col // size)
        left = [mm(t, jnp.where(below, g, 0.0)) for t, g in zip(result, grams)]
        result = [t - mm(half, t) for t, half in zip(result, left)]
        pause()
    return result


def kernel(
    c_ref, a_ref, x_ref, o_ref,
    V, C_in, Ct, gram_a, gram_l, gram_u, gram_in, t_a, t_l, t_u, g_t, h_t, b_1, b_2, m_t,
    p_own, p_in, P_own, P_in,
    ring_send, ring_recv, row_send, row_recv, chain_send, chain_recv, local_sem,
):
    row = lax.axis_index("row")
    col = lax.axis_index("col")
    last = lax.axis_size("row") - 1
    y, x = col // SIDE, col % SIDE

    def at_x(step):
        return (row, y * SIDE + (x + step + SIDE) % SIDE)

    def at_y(step):
        return (row, ((y + step + SIDE) % SIDE) * SIDE + x)

    above = ((row + last) % (last + 1), col)
    below = ((row + 1) % (last + 1), col)
    has_above = row > 0
    has_below = row < last

    def remote(src, dst, sems, index, device):
        send, recv = sems
        return pltpu.make_async_remote_copy(
            src_ref=src, dst_ref=dst, send_sem=send.at[index], recv_sem=recv.at[index],
            device_id=device, device_id_type=MESH,
        )

    ring = (ring_send, ring_recv)
    rows = (row_send, row_recv)
    chain = (chain_send, chain_recv)

    barrier = pltpu.get_barrier_semaphore()
    for device in (at_x(1), at_x(2), at_x(3), at_y(1), at_y(2), at_y(3)):
        pl.semaphore_signal(barrier, inc=1, device_id=device, device_id_type=MESH)

    @pl.when(has_above)
    def _():
        pl.semaphore_signal(barrier, inc=1, device_id=above, device_id_type=MESH)

    @pl.when(has_below)
    def _():
        pl.semaphore_signal(barrier, inc=1, device_id=below, device_id_type=MESH)

    def own_block(group, half):
        source = x_ref if group < 2 else a_ref
        return source.at[group % 2, :, pl.ds((1 - half) * NB, NB)]

    def one(group, half, k):
        if half == 0:
            return V.at[group, half, y, (x + k + SIDE) % SIDE]
        return V.at[group, half, (y + k + SIDE) % SIDE, x]

    def line(group, half, k):
        if half == 0:
            return V.at[group, half, (y + k + SIDE) % SIDE]
        return V.at[group, half, :, (x + k + SIDE) % SIDE]

    own_copies = [
        pltpu.make_async_copy(own_block(g, h), one(g, h, 0), local_sem.at[2 * g + h])
        for g in range(4) for h in range(2)
    ]
    c_copy = pltpu.make_async_copy(c_ref, C_in, local_sem.at[8])
    for copy in own_copies:
        copy.start()
    c_copy.start()

    def ring_stage(base, own, slot, device, split):
        first, second = pl.ds(0, split), pl.ds(split, split)
        return (
            remote(own, slot(0), ring, base, device(1)),
            remote(own, slot(0), ring, base + 1, device(-1)),
            remote(slot(-1).at[first], slot(-1).at[first], ring, base + 2, device(1)),
            remote(slot(1).at[second], slot(1).at[second], ring, base + 3, device(-1)),
        )

    def begin(stage):
        stage[0].start()
        stage[1].start()

    def pass_on(stage):
        stage[0].wait_recv()
        stage[2].start()
        stage[1].wait_recv()
        stage[3].start()

    def finish(stage):
        stage[2].wait_recv()
        stage[3].wait_recv()

    near, far = {}, {}
    for g in range(4):
        for h in range(2):
            base = 8 * (2 * g + h)
            axes = (at_x, at_y) if h == 0 else (at_y, at_x)
            near[g, h] = [
                remote(own_block(g, h), one(g, h, 0), ring, base + i, axes[0](k))
                for i, k in enumerate((1, -1, 2))
            ]
            far[g, h] = ring_stage(
                base + 4, line(g, h, 0), lambda k, g=g, h=h: line(g, h, k), axes[1], 2
            )

    def near_to_far(g):
        for h in range(2):
            for copy in near[g, h]:
                copy.wait_recv()
            begin(far[g, h])

    def far_pass(g):
        for h in range(2):
            pass_on(far[g, h])

    def far_finish(g):
        for h in range(2):
            finish(far[g, h])

    ends = (row + last) // (last + 1) + (2 * last - row) // (last + 1)
    pl.semaphore_wait(barrier, 6 + ends)
    for g in range(4):
        for h in range(2):
            for copy in near[g, h]:
                copy.start()

    for s in range(2):
        gram_in[s, :HALF, HALF:] = jnp.zeros((HALF, HALF), jnp.float32)
        t_u[s, :HALF, HALF:] = jnp.zeros((HALF, HALF), jnp.float32)

    @pl.when(row == last)
    def _():
        for s in range(2):
            gram_in[s, HALF:] = jnp.zeros((HALF, NB), jnp.float32)
            gram_in[s, :HALF, :HALF] = jnp.zeros((HALF, HALF), jnp.float32)
        P_in[...] = jnp.zeros_like(P_in)

    @pl.when(row == 0)
    def _():
        p_in[...] = jnp.zeros_like(p_in)

    for copy in own_copies:
        copy.wait()
    near_to_far(0)
    near_to_far(1)
    c_copy.wait()
    Ct[...] = C_in[...].T
    far_pass(0)
    near_to_far(2)
    far_pass(1)
    near_to_far(3)

    def x_up(s):
        return V[s, 1].reshape(NB, NB)

    def x_low(s):
        return V[s, 0].reshape(NB, NB)

    def a_up(s):
        return V[2 + s, 1].reshape(NB, NB)

    def a_low(s):
        return V[2 + s, 0].reshape(NB, NB)

    def triangle(source, target, s, base, device):
        return [
            remote(
                source.at[s, pl.ds(0, HALF), pl.ds(0, HALF)], target.at[s, pl.ds(0, HALF), pl.ds(0, HALF)],
                rows, base, device,
            ),
            remote(
                source.at[s, pl.ds(HALF, HALF)], target.at[s, pl.ds(HALF, HALF)], rows, base + 1, device
            ),
        ]

    gram_up = [triangle(gram_u, gram_in, s, 2 * s, above) for s in range(2)]
    t_down = [triangle(t_l, t_u, s, 4 + 2 * s, below) for s in range(2)]
    p_down = [remote(p_own.at[s], p_in.at[s], rows, 8 + s, below) for s in range(2)]
    P_up = [
        [
            remote(
                P_own.at[s, pl.ds(k * PIECE, PIECE)], P_in.at[s, pl.ds(k * PIECE, PIECE)],
                chain, s * PIECES + k, above,
            )
            for k in range(PIECES)
        ]
        for s in range(2)
    ]

    def upper_gram(s):
        gram_u[s] = mmt(x_up(s), x_up(s))

        @pl.when(has_above)
        def _():
            for copy in gram_up[s]:
                copy.start()

    def aligned_products(s):
        gram_a[s] = mmt(a_up(s), a_up(s)) + mmt(a_low(s), a_low(s))

    def cross_products(s):
        g_t[s] = mmt(x_low(s), a_low(s))
        h_t[s] = mmt(a_up(s), x_up(s))

    far_finish(0)
    upper_gram(0)
    far_finish(1)
    upper_gram(1)
    for s in range(2):
        gram_l[s] = mmt(x_low(s), x_low(s))
    p_own[0] = mmt(Ct[:, NB:], x_low(0))

    @pl.when(has_below)
    def _():
        p_down[0].start()

    far_pass(2)
    far_pass(3)
    far_finish(2)
    aligned_products(0)
    t_a[0] = lower_inverses([gram_a[0]])[0]
    cross_products(0)
    b_2[0] = mm(t_a[0], h_t[0])
    far_finish(3)
    aligned_products(1)
    cross_products(1)

    @pl.when(has_below)
    def _():
        for s in range(2):
            for copy in gram_up[s]:
                copy.wait_recv()

    three = lower_inverses([gram_l[0] + gram_in[0], gram_l[1] + gram_in[1], gram_a[1]])
    for s in range(2):
        t_l[s] = three[s]

        @pl.when(has_below)
        def _():
            for copy in t_down[s]:
                copy.start()

    t_a[1] = three[2]
    b_2[1] = mm(t_a[1], h_t[1])
    for s in range(2):
        b_1[s] = mm(t_l[s], g_t[s])
        m_t[s] = mm(b_1[s], b_2[s])

    @pl.when(row == 0)
    def _():
        own = lower_inverses([gram_u[0], gram_u[1]])
        for s in range(2):
            t_u[s] = own[s]

    for s in range(2):
        upper, lower = Ct[:, :NB], Ct[:, NB:]
        w = mmt(upper, a_up(s)) + mmt(lower, a_low(s))
        P_own[s] = mmt(upper, x_up(s)) - mm(w, b_2[s]) + mm(p_own[s], m_t[s])
        for k in range(PIECES):
            piece = pl.ds(k * PIECE, PIECE)

            @pl.when(has_below)
            def _():
                P_up[s][k].wait_recv()
                P_own[s, piece] += mm(P_in[s, piece], m_t[s])

            @pl.when(has_above)
            def _():
                P_up[s][k].start()

        both = p_own[s] + P_in[s]
        coeffs_a = mm(w - mm(both, b_1[s]), t_a[s])
        coeffs_l = mm(both, t_l[s])
        Ct[:, NB:] = lower - mm(coeffs_l, x_low(s)) - mm(coeffs_a, a_low(s))
        if s == 0:
            p_own[1] = mmt(Ct[:, NB:], x_low(1))

            @pl.when(has_below)
            def _():
                p_down[1].start()

        @pl.when(has_above)
        def _():
            p_down[s].wait_recv()
            for copy in t_down[s]:
                copy.wait_recv()

        coeffs_u = mm(p_in[s] + P_own[s], t_u[s])
        Ct[:, :NB] = upper - mm(coeffs_a, a_up(s)) - mm(coeffs_u, x_up(s))

    o_ref[...] = Ct[...].T

    for stages in (near, far):
        for stage in stages.values():
            for copy in stage:
                copy.wait_send()

    @pl.when(has_above)
    def _():
        for copy in gram_up[0] + gram_up[1] + P_up[0] + P_up[1]:
            copy.wait_send()

    @pl.when(has_below)
    def _():
        for copy in t_down[0] + t_down[1] + p_down:
            copy.wait_send()


def on_device(eigenvectors, aligned_vectors, straddle_vectors):
    columns = eigenvectors.shape[1]
    in_place = pl.BlockSpec(memory_space=pl.ANY)
    square = pltpu.VMEM((2, NB, NB), jnp.float32)
    product = pltpu.VMEM((2, columns, NB), jnp.float32)
    dma = pltpu.SemaphoreType.DMA
    return pl.pallas_call(
        kernel,
        out_shape=jax.ShapeDtypeStruct(eigenvectors.shape, jnp.float32),
        in_specs=[in_place] * 3,
        out_specs=pl.BlockSpec(memory_space=pltpu.VMEM),
        scratch_shapes=[
            pltpu.VMEM((4, 2, SIDE, SIDE, NB // SIDE**2, NB), jnp.float32),
            pltpu.VMEM(eigenvectors.shape, jnp.float32),
            pltpu.VMEM((columns, SPAN), jnp.float32),
        ]
        + [square] * 12
        + [product] * 4
        + [dma((64,)), dma((64,)), dma((10,)), dma((10,)), dma((2 * PIECES,)), dma((2 * PIECES,)), dma((9,))],
        compiler_params=pltpu.CompilerParams(
            collective_id=0, has_side_effects=True, vmem_limit_bytes=56 * 1024 * 1024
        ),
    )(
        eigenvectors,
        jnp.swapaxes(aligned_vectors, 1, 2),
        jnp.swapaxes(straddle_vectors, 1, 2),
    )


def solution(mesh):
    placed = (P("row", "col"), P(None, "row", "col"), P(None, "row", "col"))
    return jax.shard_map(
        on_device, mesh=mesh, in_specs=placed, out_specs=P("row", "col"), check_vma=False
    )
```

```python
import jax
import jax.numpy as jnp
from jax import lax
from jax.experimental import pallas as pl
from jax.experimental.pallas import tpu as pltpu
from jax.sharding import PartitionSpec as P

NB = 256
SPAN = 2 * NB
HALF = NB // 2
SIDE = 4
PIECES = 4
PIECE = 32
MESH = pl.DeviceIdType.MESH
HIGH = lax.Precision.HIGH


def mm(left, right):
    return lax.dot_general(
        left, right, (((1,), (0,)), ((), ())), precision=HIGH, preferred_element_type=jnp.float32
    )


def mmt(left, right):
    return lax.dot_general(
        left, right, (((1,), (1,)), ((), ())), precision=HIGH, preferred_element_type=jnp.float32
    )


def lower_inverses(grams, between=()):
    between = list(between)

    def pause():
        if between:
            between.pop(0)()

    row = lax.broadcasted_iota(jnp.int32, (NB, NB), 0)
    col = lax.broadcasted_iota(jnp.int32, (NB, NB), 1)
    on_diagonal = row == col
    eye = jnp.where(on_diagonal, 1.0, 0.0)
    small = (row // 32 == col // 32) & (row > col)
    down = [0.5 * jnp.sum(jnp.where(on_diagonal, g, 0.0), axis=1, keepdims=True) for g in grams]
    across = [0.5 * jnp.sum(jnp.where(on_diagonal, g, 0.0), axis=0, keepdims=True) for g in grams]
    powers = [jnp.where(small, g, 0.0) / d for g, d in zip(grams, down)]
    result = [eye - n for n in powers]
    for _ in range(4):
        powers = [mm(n, n) for n in powers]
        result = [t + mm(t, n) for t, n in zip(result, powers)]
    pause()
    result = [t / d for t, d in zip(result, across)]
    for size in (32, 64, 128):
        below = (row // (2 * size) == col // (2 * size)) & (row // size > col // size)
        left = [mm(t, jnp.where(below, g, 0.0)) for t, g in zip(result, grams)]
        result = [t - mm(half, t) for t, half in zip(result, left)]
        pause()
    return result


def kernel(
    c_ref, a_ref, x_ref, o_ref,
    V, C_in, Ct, gram_a, gram_l, gram_u, gram_in, gram_low, t_a, t_l, t_u, g_t, b_1, b_2, m_t,
    p_own, p_in, P_own, P_in,
    ring_send, ring_recv, row_send, row_recv, chain_send, chain_recv, local_sem,
):
    row = lax.axis_index("row")
    col = lax.axis_index("col")
    last = lax.axis_size("row") - 1
    y, x = col // SIDE, col % SIDE

    def at_x(step):
        return (row, y * SIDE + (x + step + SIDE) % SIDE)

    def at_y(step):
        return (row, ((y + step + SIDE) % SIDE) * SIDE + x)

    above = ((row + last) % (last + 1), col)
    below = ((row + 1) % (last + 1), col)
    second = last - 1
    has_above = row > 0
    has_below = row < last

    def remote(src, dst, sems, index, device):
        send, recv = sems
        return pltpu.make_async_remote_copy(
            src_ref=src, dst_ref=dst, send_sem=send.at[index], recv_sem=recv.at[index],
            device_id=device, device_id_type=MESH,
        )

    ring = (ring_send, ring_recv)
    rows = (row_send, row_recv)
    chain = (chain_send, chain_recv)

    barrier = pltpu.get_barrier_semaphore()
    for device in (at_x(1), at_x(2), at_x(3), at_y(1), at_y(2), at_y(3)):
        pl.semaphore_signal(barrier, inc=1, device_id=device, device_id_type=MESH)

    @pl.when(has_above)
    def _():
        pl.semaphore_signal(barrier, inc=1, device_id=above, device_id_type=MESH)

    @pl.when(has_below)
    def _():
        pl.semaphore_signal(barrier, inc=1, device_id=below, device_id_type=MESH)

    def own_block(group, half):
        source = a_ref if group < 2 else x_ref
        return source.at[group % 2, :, pl.ds((1 - half) * NB, NB)]

    def one(group, half, k):
        if half == 0:
            return V.at[group, half, y, (x + k + SIDE) % SIDE]
        return V.at[group, half, (y + k + SIDE) % SIDE, x]

    def line(group, half, k):
        if half == 0:
            return V.at[group, half, (y + k + SIDE) % SIDE]
        return V.at[group, half, :, (x + k + SIDE) % SIDE]

    own_copies = [
        pltpu.make_async_copy(own_block(g, h), one(g, h, 0), local_sem.at[2 * g + h])
        for g in range(4) for h in range(2)
    ]
    c_copy = pltpu.make_async_copy(c_ref, C_in, local_sem.at[8])
    for copy in own_copies:
        copy.start()
    c_copy.start()

    def ring_stage(base, own, slot, device, split):
        first, second = pl.ds(0, split), pl.ds(split, split)
        return (
            remote(own, slot(0), ring, base, device(1)),
            remote(own, slot(0), ring, base + 1, device(-1)),
            remote(slot(-1).at[first], slot(-1).at[first], ring, base + 2, device(1)),
            remote(slot(1).at[second], slot(1).at[second], ring, base + 3, device(-1)),
        )

    def begin(stage):
        stage[0].start()
        stage[1].start()

    def pass_on(stage):
        stage[0].wait_recv()
        stage[2].start()
        stage[1].wait_recv()
        stage[3].start()

    def finish(stage):
        stage[2].wait_recv()
        stage[3].wait_recv()

    near, far = {}, {}
    for g in range(4):
        for h in range(2):
            base = 8 * (2 * g + h)
            axes = (at_x, at_y) if h == 0 else (at_y, at_x)
            near[g, h] = [
                remote(own_block(g, h), one(g, h, 0), ring, base + i, axes[0](k))
                for i, k in enumerate((1, -1, 2))
            ]
            far[g, h] = ring_stage(
                base + 4, line(g, h, 0), lambda k, g=g, h=h: line(g, h, k), axes[1], 2
            )

    def near_to_far(g):
        for h in range(2):
            for copy in near[g, h]:
                copy.wait_recv()
            begin(far[g, h])

    def far_pass(g):
        for h in range(2):
            pass_on(far[g, h])

    def far_finish(g):
        for h in range(2):
            finish(far[g, h])

    ends = (row + last) // (last + 1) + (2 * last - row) // (last + 1)
    pl.semaphore_wait(barrier, 6 + ends)
    for g in range(4):
        for h in range(2):
            for copy in near[g, h]:
                copy.start()

    gram_low[0, :HALF, HALF:] = jnp.zeros((HALF, HALF), jnp.float32)
    for s in range(2):
        gram_in[s, :HALF, HALF:] = jnp.zeros((HALF, HALF), jnp.float32)
        t_u[s, :HALF, HALF:] = jnp.zeros((HALF, HALF), jnp.float32)

    @pl.when(row == last)
    def _():
        for s in range(2):
            gram_in[s, HALF:] = jnp.zeros((HALF, NB), jnp.float32)
            gram_in[s, :HALF, :HALF] = jnp.zeros((HALF, HALF), jnp.float32)
        P_in[...] = jnp.zeros_like(P_in)

    @pl.when(row == 0)
    def _():
        p_in[...] = jnp.zeros_like(p_in)

    for copy in own_copies:
        copy.wait()
    near_to_far(0)
    near_to_far(1)
    c_copy.wait()
    Ct[...] = C_in[...].T
    far_pass(0)
    near_to_far(2)
    far_pass(1)
    near_to_far(3)

    def x_up(s):
        return V[2 + s, 1].reshape(NB, NB)

    def x_low(s):
        return V[2 + s, 0].reshape(NB, NB)

    def a_up(s):
        return V[s, 1].reshape(NB, NB)

    def a_low(s):
        return V[s, 0].reshape(NB, NB)

    def triangle(source, target, s, base, device):
        return [
            remote(
                source.at[s, pl.ds(0, HALF), pl.ds(0, HALF)], target.at[s, pl.ds(0, HALF), pl.ds(0, HALF)],
                rows, base, device,
            ),
            remote(
                source.at[s, pl.ds(HALF, HALF)], target.at[s, pl.ds(HALF, HALF)], rows, base + 1, device
            ),
        ]

    gram_up = [triangle(gram_u, gram_in, s, 2 * s, above) for s in range(2)]
    t_down = [triangle(t_l, t_u, s, 4 + 2 * s, below) for s in range(2)]
    p_down = [remote(p_own.at[s], p_in.at[s], rows, 8 + s, below) for s in range(2)]
    P_up = [
        [
            remote(
                P_own.at[s, pl.ds(k * PIECE, PIECE)], P_in.at[s, pl.ds(k * PIECE, PIECE)],
                chain, s * PIECES + k, above,
            )
            for k in range(PIECES)
        ]
        for s in range(2)
    ]

    low_down = triangle(gram_l, gram_low, 0, 10, below)

    def upper_gram(s):
        gram_u[s] = mmt(x_up(s), x_up(s))

        @pl.when(has_above)
        def _():
            for copy in gram_up[s]:
                copy.start()

    def lower_gram(s):
        gram_l[s] = mmt(x_low(s), x_low(s))

    def first_x():
        far_finish(2)
        lower_gram(0)

        @pl.when(row == second - 1)
        def _():
            for copy in low_down:
                copy.start()

        upper_gram(0)

    for s in range(2):
        far_finish(s)
        gram_a[s] = mmt(a_up(s), a_up(s)) + mmt(a_low(s), a_low(s))
        if s == 0:
            far_pass(2)
    pair = lower_inverses([gram_a[0], gram_a[1]], (lambda: far_pass(3), first_x))
    for s in range(2):
        t_a[s] = pair[s]
    p_own[0] = mmt(Ct[:, NB:], x_low(0))

    @pl.when(has_below)
    def _():
        p_down[0].start()

    far_finish(3)
    upper_gram(1)
    lower_gram(1)
    for s in range(2):
        g_t[s] = mmt(x_low(s), a_low(s))
        b_2[s] = mm(t_a[s], mmt(a_up(s), x_up(s)))

    @pl.when(has_below)
    def _():
        for s in range(2):
            for copy in gram_up[s]:
                copy.wait_recv()


    @pl.when(row == second)
    def _():
        for copy in low_down:
            copy.wait_recv()
        three = lower_inverses(
            [gram_l[0] + gram_in[0], gram_l[1] + gram_in[1], gram_u[0] + gram_low[0]]
        )
        t_l[0] = three[0]
        t_l[1] = three[1]
        t_u[0] = three[2]

    @pl.when(row != second)
    def _():
        two = lower_inverses([gram_l[0] + gram_in[0], gram_l[1] + gram_in[1]])
        t_l[0] = two[0]
        t_l[1] = two[1]

    sends_first = has_below & (row != second - 1)
    takes_first = has_above & (row != second)

    @pl.when(sends_first)
    def _():
        for copy in t_down[0]:
            copy.start()

    @pl.when(has_below)
    def _():
        for copy in t_down[1]:
            copy.start()

    for s in range(2):
        b_1[s] = mm(t_l[s], g_t[s])
        m_t[s] = mm(b_1[s], b_2[s])

    @pl.when(row == 0)
    def _():
        own = lower_inverses([gram_u[0], gram_u[1]])
        for s in range(2):
            t_u[s] = own[s]

    for s in range(2):
        upper, lower = Ct[:, :NB], Ct[:, NB:]
        w = mmt(upper, a_up(s)) + mmt(lower, a_low(s))
        P_own[s] = mmt(upper, x_up(s)) - mm(w, b_2[s]) + mm(p_own[s], m_t[s])
        for k in range(PIECES):
            piece = pl.ds(k * PIECE, PIECE)

            @pl.when(has_below)
            def _():
                P_up[s][k].wait_recv()
                P_own[s, piece] += mm(P_in[s, piece], m_t[s])

            @pl.when(has_above)
            def _():
                P_up[s][k].start()

        both = p_own[s] + P_in[s]
        coeffs_a = mm(w - mm(both, b_1[s]), t_a[s])
        coeffs_l = mm(both, t_l[s])
        Ct[:, NB:] = lower - mm(coeffs_l, x_low(s)) - mm(coeffs_a, a_low(s))
        if s == 0:
            p_own[1] = mmt(Ct[:, NB:], x_low(1))

            @pl.when(has_below)
            def _():
                p_down[1].start()

        @pl.when(has_above)
        def _():
            p_down[s].wait_recv()

        @pl.when(takes_first if s == 0 else has_above)
        def _():
            for copy in t_down[s]:
                copy.wait_recv()

        coeffs_u = mm(p_in[s] + P_own[s], t_u[s])
        Ct[:, :NB] = upper - mm(coeffs_a, a_up(s)) - mm(coeffs_u, x_up(s))

    o_ref[...] = Ct[...].T

    for stages in (near, far):
        for stage in stages.values():
            for copy in stage:
                copy.wait_send()

    @pl.when(has_above)
    def _():
        for copy in gram_up[0] + gram_up[1] + P_up[0] + P_up[1]:
            copy.wait_send()

    @pl.when(has_below)
    def _():
        for copy in t_down[1] + p_down:
            copy.wait_send()

    @pl.when(sends_first)
    def _():
        for copy in t_down[0]:
            copy.wait_send()

    @pl.when(row == second - 1)
    def _():
        for copy in low_down:
            copy.wait_send()


def on_device(eigenvectors, aligned_vectors, straddle_vectors):
    columns = eigenvectors.shape[1]
    in_place = pl.BlockSpec(memory_space=pltpu.HBM)
    square = pltpu.VMEM((2, NB, NB), jnp.float32)
    product = pltpu.VMEM((2, columns, NB), jnp.float32)
    dma = pltpu.SemaphoreType.DMA
    return pl.pallas_call(
        kernel,
        out_shape=jax.ShapeDtypeStruct(eigenvectors.shape, jnp.float32),
        in_specs=[in_place] * 3,
        out_specs=pl.BlockSpec(memory_space=pltpu.VMEM),
        scratch_shapes=[
            pltpu.VMEM((4, 2, SIDE, SIDE, NB // SIDE**2, NB), jnp.float32),
            pltpu.VMEM(eigenvectors.shape, jnp.float32),
            pltpu.VMEM((columns, SPAN), jnp.float32),
        ]
        + [square] * 12
        + [product] * 4
        + [dma((64,)), dma((64,)), dma((12,)), dma((12,)), dma((2 * PIECES,)), dma((2 * PIECES,)), dma((9,))],
        compiler_params=pltpu.CompilerParams(
            collective_id=0, has_side_effects=True, vmem_limit_bytes=40 * 1024 * 1024
        ),
    )(
        pltpu.with_memory_space_constraint(eigenvectors, pltpu.HBM),
        pltpu.with_memory_space_constraint(jnp.swapaxes(aligned_vectors, 1, 2), pltpu.HBM),
        pltpu.with_memory_space_constraint(jnp.swapaxes(straddle_vectors, 1, 2), pltpu.HBM),
    )


def solution(mesh):
    placed = (P("row", "col"), P(None, "row", "col"), P(None, "row", "col"))
    return jax.shard_map(
        on_device, mesh=mesh, in_specs=placed, out_specs=P("row", "col"), check_vma=False
    )
```

```python
import jax
import jax.numpy as jnp
from jax import lax
from jax.experimental import pallas as pl
from jax.experimental.pallas import tpu as pltpu
from jax.sharding import PartitionSpec as P

NB = 256
SPAN = 2 * NB
HALF = NB // 2
SIDE = 4
PIECES = 4
PIECE = 32
MESH = pl.DeviceIdType.MESH
HIGH = lax.Precision.HIGH


def mm(left, right):
    return lax.dot_general(
        left, right, (((1,), (0,)), ((), ())), precision=HIGH, preferred_element_type=jnp.float32
    )


def mmt(left, right):
    return lax.dot_general(
        left, right, (((1,), (1,)), ((), ())), precision=HIGH, preferred_element_type=jnp.float32
    )


def lower_inverses(grams):
    row = lax.broadcasted_iota(jnp.int32, (NB, NB), 0)
    col = lax.broadcasted_iota(jnp.int32, (NB, NB), 1)
    on_diagonal = row == col
    eye = jnp.where(on_diagonal, 1.0, 0.0)
    small = (row // 32 == col // 32) & (row > col)
    down = [0.5 * jnp.sum(jnp.where(on_diagonal, g, 0.0), axis=1, keepdims=True) for g in grams]
    across = [0.5 * jnp.sum(jnp.where(on_diagonal, g, 0.0), axis=0, keepdims=True) for g in grams]
    powers = [jnp.where(small, g, 0.0) / d for g, d in zip(grams, down)]
    result = [eye - n for n in powers]
    for _ in range(4):
        powers = [mm(n, n) for n in powers]
        result = [t + mm(t, n) for t, n in zip(result, powers)]
    result = [t / d for t, d in zip(result, across)]
    for size in (32, 64, 128):
        below = (row // (2 * size) == col // (2 * size)) & (row // size > col // size)
        left = [mm(t, jnp.where(below, g, 0.0)) for t, g in zip(result, grams)]
        result = [t - mm(half, t) for t, half in zip(result, left)]
    return result


def kernel(
    c_ref, a_ref, x_ref, o_ref,
    V, C_in, Ct, gram_a, gram_l, gram_u, gram_in, t_a, t_l, t_u, g_t, b_1, b_2, m_t,
    p_own, p_in, P_own, P_in, w_own,
    ring_send, ring_recv, row_send, row_recv, chain_send, chain_recv, local_sem,
):
    row = lax.axis_index("row")
    col = lax.axis_index("col")
    last = lax.axis_size("row") - 1
    y, x = col // SIDE, col % SIDE

    def at_x(step):
        return (row, y * SIDE + (x + step + SIDE) % SIDE)

    def at_y(step):
        return (row, ((y + step + SIDE) % SIDE) * SIDE + x)

    above = ((row + last) % (last + 1), col)
    below = ((row + 1) % (last + 1), col)
    has_above = row > 0
    has_below = row < last

    def remote(src, dst, sems, index, device):
        send, recv = sems
        return pltpu.make_async_remote_copy(
            src_ref=src, dst_ref=dst, send_sem=send.at[index], recv_sem=recv.at[index],
            device_id=device, device_id_type=MESH,
        )

    ring = (ring_send, ring_recv)
    rows = (row_send, row_recv)
    chain = (chain_send, chain_recv)

    barrier = pltpu.get_barrier_semaphore()
    for device in (at_x(1), at_x(2), at_x(3), at_y(1), at_y(2), at_y(3)):
        pl.semaphore_signal(barrier, inc=1, device_id=device, device_id_type=MESH)

    @pl.when(has_above)
    def _():
        pl.semaphore_signal(barrier, inc=1, device_id=above, device_id_type=MESH)

    @pl.when(has_below)
    def _():
        pl.semaphore_signal(barrier, inc=1, device_id=below, device_id_type=MESH)

    def own_block(group, half):
        upper, lower = pl.ds(0, NB), pl.ds(NB, NB)
        if group == 0:
            return x_ref.at[half, :, upper]
        if group == 3:
            return x_ref.at[half, :, lower]
        return a_ref.at[group - 1, :, upper if half == 1 else lower]

    def one(group, half, k):
        if half == 0:
            return V.at[group, half, y, (x + k + SIDE) % SIDE]
        return V.at[group, half, (y + k + SIDE) % SIDE, x]

    def line(group, half, k):
        if half == 0:
            return V.at[group, half, (y + k + SIDE) % SIDE]
        return V.at[group, half, :, (x + k + SIDE) % SIDE]

    own_copies = [
        pltpu.make_async_copy(own_block(g, h), one(g, h, 0), local_sem.at[2 * g + h])
        for g in range(4) for h in range(2)
    ]
    c_copy = pltpu.make_async_copy(c_ref, C_in, local_sem.at[8])
    for copy in own_copies:
        copy.start()
    c_copy.start()

    def ring_stage(base, own, slot, device, split):
        first, second = pl.ds(0, split), pl.ds(split, split)
        return (
            remote(own, slot(0), ring, base, device(1)),
            remote(own, slot(0), ring, base + 1, device(-1)),
            remote(slot(-1).at[first], slot(-1).at[first], ring, base + 2, device(1)),
            remote(slot(1).at[second], slot(1).at[second], ring, base + 3, device(-1)),
        )

    def begin(stage):
        stage[0].start()
        stage[1].start()

    def pass_on(stage):
        stage[0].wait_recv()
        stage[2].start()
        stage[1].wait_recv()
        stage[3].start()

    def finish(stage):
        stage[2].wait_recv()
        stage[3].wait_recv()

    near, far = {}, {}
    for g in range(4):
        for h in range(2):
            base = 8 * (2 * g + h)
            axes = (at_x, at_y) if h == 0 else (at_y, at_x)
            near[g, h] = [
                remote(own_block(g, h), one(g, h, 0), ring, base + i, axes[0](k))
                for i, k in enumerate((1, -1, 2))
            ]
            far[g, h] = ring_stage(
                base + 4, line(g, h, 0), lambda k, g=g, h=h: line(g, h, k), axes[1], 2
            )

    def near_to_far(g):
        for h in range(2):
            for copy in near[g, h]:
                copy.wait_recv()
            begin(far[g, h])

    def far_pass(g):
        for h in range(2):
            pass_on(far[g, h])

    def far_finish(g):
        for h in range(2):
            finish(far[g, h])

    ends = (row + last) // (last + 1) + (2 * last - row) // (last + 1)
    pl.semaphore_wait(barrier, 6 + ends)
    for g in range(4):
        for h in range(2):
            for copy in near[g, h]:
                copy.start()

    for s in range(2):
        gram_in[s, :HALF, HALF:] = jnp.zeros((HALF, HALF), jnp.float32)
        t_u[s, :HALF, HALF:] = jnp.zeros((HALF, HALF), jnp.float32)

    @pl.when(row == last)
    def _():
        for s in range(2):
            gram_in[s, HALF:] = jnp.zeros((HALF, NB), jnp.float32)
            gram_in[s, :HALF, :HALF] = jnp.zeros((HALF, HALF), jnp.float32)
        P_in[...] = jnp.zeros_like(P_in)

    @pl.when(row == 0)
    def _():
        p_in[...] = jnp.zeros_like(p_in)

    for copy in own_copies:
        copy.wait()
    near_to_far(0)
    near_to_far(1)
    c_copy.wait()
    Ct[...] = C_in[...].T
    far_pass(0)
    near_to_far(2)
    far_pass(1)
    near_to_far(3)

    def x_up(s):
        return V[0, s].reshape(NB, NB)

    def x_low(s):
        return V[3, s].reshape(NB, NB)

    def a_up(s):
        return V[1 + s, 1].reshape(NB, NB)

    def a_low(s):
        return V[1 + s, 0].reshape(NB, NB)

    def triangle(source, target, s, base, device):
        return [
            remote(
                source.at[s, pl.ds(0, HALF), pl.ds(0, HALF)], target.at[s, pl.ds(0, HALF), pl.ds(0, HALF)],
                rows, base, device,
            ),
            remote(
                source.at[s, pl.ds(HALF, HALF)], target.at[s, pl.ds(HALF, HALF)], rows, base + 1, device
            ),
        ]

    gram_up = [triangle(gram_u, gram_in, s, 2 * s, above) for s in range(2)]
    t_down = [triangle(t_l, t_u, s, 4 + 2 * s, below) for s in range(2)]
    p_down = [remote(p_own.at[s], p_in.at[s], rows, 8 + s, below) for s in range(2)]
    P_up = [
        [
            remote(
                P_own.at[s, pl.ds(k * PIECE, PIECE)], P_in.at[s, pl.ds(k * PIECE, PIECE)],
                chain, s * PIECES + k, above,
            )
            for k in range(PIECES)
        ]
        for s in range(2)
    ]


    def upper_gram(s):
        gram_u[s] = mmt(x_up(s), x_up(s))

        @pl.when(has_above)
        def _():
            for copy in gram_up[s]:
                copy.start()

    far_finish(0)
    for s in range(2):
        upper_gram(s)
    far_pass(2)
    far_finish(1)
    gram_a[0] = mmt(a_up(0), a_up(0)) + mmt(a_low(0), a_low(0))
    far_pass(3)
    far_finish(2)
    gram_a[1] = mmt(a_up(1), a_up(1)) + mmt(a_low(1), a_low(1))
    pair = lower_inverses([gram_a[0], gram_a[1]])
    for s in range(2):
        t_a[s] = pair[s]
        b_2[s] = mm(t_a[s], mmt(a_up(s), x_up(s)))

    def local_part(s):
        upper, lower = Ct[:, :NB], Ct[:, NB:]
        w_own[...] = mmt(upper, a_up(s)) + mmt(lower, a_low(s))
        P_own[s] = mmt(upper, x_up(s)) - mm(w_own[...], b_2[s])

    local_part(0)
    far_finish(3)
    gram_l[0] = mmt(x_low(0), x_low(0))

    gram_l[1] = mmt(x_low(1), x_low(1))
    p_own[0] = mmt(Ct[:, NB:], x_low(0))

    @pl.when(has_below)
    def _():
        p_down[0].start()
        for s in range(2):
            for copy in gram_up[s]:
                copy.wait_recv()

    for s in range(2):
        g_t[s] = mmt(x_low(s), a_low(s))
    pair = lower_inverses([gram_l[0] + gram_in[0], gram_l[1] + gram_in[1]])
    for s in range(2):
        t_l[s] = pair[s]

    @pl.when(has_below)
    def _():
        for copy in t_down[0] + t_down[1]:
            copy.start()

    for s in range(2):
        b_1[s] = mm(t_l[s], g_t[s])
        m_t[s] = mm(b_1[s], b_2[s])

    @pl.when(row == 0)
    def _():
        own = lower_inverses([gram_u[0], gram_u[1]])
        for s in range(2):
            t_u[s] = own[s]

    P_own[0] += mm(p_own[0], m_t[0])
    for s in range(2):
        for k in range(PIECES):
            piece = pl.ds(k * PIECE, PIECE)

            @pl.when(has_below)
            def _():
                P_up[s][k].wait_recv()
                P_own[s, piece] += mm(P_in[s, piece], m_t[s])

            @pl.when(has_above)
            def _():
                P_up[s][k].start()

        if s == 0:

            @pl.when(has_above)
            def _():
                for copy in t_down[0] + [p_down[0]]:
                    copy.wait_recv()

        both = p_own[s] + P_in[s]
        coeffs_a = mm(w_own[...] - mm(both, b_1[s]), t_a[s])
        coeffs_l = mm(both, t_l[s])
        upper, lower = Ct[:, :NB], Ct[:, NB:]
        lower = lower - mm(coeffs_l, x_low(s)) - mm(coeffs_a, a_low(s))
        upper = upper - mm(coeffs_a, a_up(s))
        if s == 1:

            @pl.when(has_above)
            def _():
                for copy in t_down[1] + [p_down[1]]:
                    copy.wait_recv()

        upper = upper - mm(mm(p_in[s] + P_own[s], t_u[s]), x_up(s))
        Ct[:, NB:] = lower
        Ct[:, :NB] = upper
        if s == 0:
            p_own[1] = mmt(lower, x_low(1))
            local_part(1)
            P_own[1] += mm(p_own[1], m_t[1])

            @pl.when(has_below)
            def _():
                p_down[1].start()

    o_ref[...] = Ct[...].T

    for stages in (near, far):
        for stage in stages.values():
            for copy in stage:
                copy.wait_send()

    @pl.when(has_above)
    def _():
        for copy in gram_up[0] + gram_up[1] + P_up[0] + P_up[1]:
            copy.wait_send()

    @pl.when(has_below)
    def _():
        for copy in t_down[0] + t_down[1] + p_down:
            copy.wait_send()


def on_device(eigenvectors, aligned_vectors, straddle_vectors):
    columns = eigenvectors.shape[1]
    in_place = pl.BlockSpec(memory_space=pltpu.HBM)
    square = pltpu.VMEM((2, NB, NB), jnp.float32)
    product = pltpu.VMEM((2, columns, NB), jnp.float32)
    dma = pltpu.SemaphoreType.DMA
    return pl.pallas_call(
        kernel,
        out_shape=jax.ShapeDtypeStruct(eigenvectors.shape, jnp.float32),
        in_specs=[in_place] * 3,
        out_specs=pl.BlockSpec(memory_space=pltpu.VMEM),
        scratch_shapes=[
            pltpu.VMEM((4, 2, SIDE, SIDE, NB // SIDE**2, NB), jnp.float32),
            pltpu.VMEM(eigenvectors.shape, jnp.float32),
            pltpu.VMEM((columns, SPAN), jnp.float32),
        ]
        + [square] * 11
        + [product] * 4
        + [pltpu.VMEM((columns, NB), jnp.float32)]
        + [dma((64,)), dma((64,)), dma((10,)), dma((10,)), dma((2 * PIECES,)), dma((2 * PIECES,)), dma((9,))],
        compiler_params=pltpu.CompilerParams(
            collective_id=0, has_side_effects=True, vmem_limit_bytes=40 * 1024 * 1024
        ),
    )(
        pltpu.with_memory_space_constraint(eigenvectors, pltpu.HBM),
        pltpu.with_memory_space_constraint(jnp.swapaxes(aligned_vectors, 1, 2), pltpu.HBM),
        pltpu.with_memory_space_constraint(jnp.swapaxes(straddle_vectors, 1, 2), pltpu.HBM),
    )


def solution(mesh):
    placed = (P("row", "col"), P(None, "row", "col"), P(None, "row", "col"))
    return jax.shard_map(
        on_device, mesh=mesh, in_specs=placed, out_specs=P("row", "col"), check_vma=False
    )
```

```python
import jax
import jax.numpy as jnp
from jax import lax
from jax.experimental import pallas as pl
from jax.experimental.pallas import tpu as pltpu
from jax.sharding import PartitionSpec as P

NB = 256
SPAN = 2 * NB
HALF = NB // 2
SIDE = 4
PIECES = 4
PIECE = 32
GROUP = 4
MESH = pl.DeviceIdType.MESH
HIGH = lax.Precision.HIGH


def mm(left, right):
    return lax.dot_general(
        left, right, (((1,), (0,)), ((), ())), precision=HIGH, preferred_element_type=jnp.float32
    )


def mmt(left, right):
    return lax.dot_general(
        left, right, (((1,), (1,)), ((), ())), precision=HIGH, preferred_element_type=jnp.float32
    )


def lower_inverses(grams):
    row = lax.broadcasted_iota(jnp.int32, (NB, NB), 0)
    col = lax.broadcasted_iota(jnp.int32, (NB, NB), 1)
    on_diagonal = row == col
    eye = jnp.where(on_diagonal, 1.0, 0.0)
    small = (row // 32 == col // 32) & (row > col)
    down = [0.5 * jnp.sum(jnp.where(on_diagonal, g, 0.0), axis=1, keepdims=True) for g in grams]
    across = [0.5 * jnp.sum(jnp.where(on_diagonal, g, 0.0), axis=0, keepdims=True) for g in grams]
    powers = [jnp.where(small, g, 0.0) / d for g, d in zip(grams, down)]
    result = [eye - n for n in powers]
    for _ in range(4):
        powers = [mm(n, n) for n in powers]
        result = [t + mm(t, n) for t, n in zip(result, powers)]
    result = [t / d for t, d in zip(result, across)]
    for size in (32, 64, 128):
        below = (row // (2 * size) == col // (2 * size)) & (row // size > col // size)
        left = [mm(t, jnp.where(below, g, 0.0)) for t, g in zip(result, grams)]
        result = [t - mm(half, t) for t, half in zip(result, left)]
    return result


def kernel(
    c_ref, a_ref, x_ref, o_ref,
    V, C_in, Ct, gram_a, gram_l, gram_u, gram_in, t_a, t_l, t_u, g_t, b_1, b_2, m_t,
    n_own, n_in, p_own, p_in, P_own, q_own, q_in, Z, w_own, total,
    ring_send, ring_recv, row_send, row_recv, chain_send, chain_recv, jump_send, jump_recv, local_sem,
):
    row = lax.axis_index("row")
    col = lax.axis_index("col")
    last = lax.axis_size("row") - 1
    y, x = col // SIDE, col % SIDE

    def at_x(step):
        return (row, y * SIDE + (x + step + SIDE) % SIDE)

    def at_y(step):
        return (row, ((y + step + SIDE) % SIDE) * SIDE + x)

    above = ((row + last) % (last + 1), col)
    below = ((row + 1) % (last + 1), col)
    rank, group_at = row % GROUP, row // GROUP
    groups = (last + 1) // GROUP
    is_top, is_bottom = rank == GROUP - 1, rank == 0
    has_source = group_at < groups - 1
    source = ((group_at * GROUP + GROUP) % (last + 1), col)

    partner = (row + 1 - 2 * (row % 2), col)
    hands_on = has_source & (is_top | is_bottom)

    def up(distance):
        return ((row + last + 1 - distance) % (last + 1), col)

    has_above = row > 0
    has_below = row < last

    def remote(src, dst, sems, index, device):
        send, recv = sems
        return pltpu.make_async_remote_copy(
            src_ref=src, dst_ref=dst, send_sem=send.at[index], recv_sem=recv.at[index],
            device_id=device, device_id_type=MESH,
        )

    ring = (ring_send, ring_recv)
    rows = (row_send, row_recv)
    chain = (chain_send, chain_recv)

    barrier = pltpu.get_barrier_semaphore()
    for device in (at_x(1), at_x(2), at_x(3), at_y(1), at_y(2), at_y(3)):
        pl.semaphore_signal(barrier, inc=1, device_id=device, device_id_type=MESH)

    @pl.when(has_above)
    def _():
        pl.semaphore_signal(barrier, inc=1, device_id=above, device_id_type=MESH)

    @pl.when(has_below)
    def _():
        pl.semaphore_signal(barrier, inc=1, device_id=below, device_id_type=MESH)

    sends_jump = is_bottom & has_above

    @pl.when(sends_jump)
    def _():
        pl.semaphore_signal(barrier, inc=1, device_id=up(GROUP), device_id_type=MESH)

    @pl.when(has_source & is_bottom)
    def _():
        pl.semaphore_signal(barrier, inc=1, device_id=source, device_id_type=MESH)

    def own_block(group, half):
        upper, lower = pl.ds(0, NB), pl.ds(NB, NB)
        if group == 0:
            return x_ref.at[half, :, upper]
        if group == 3:
            return x_ref.at[half, :, lower]
        return a_ref.at[group - 1, :, upper if half == 1 else lower]

    def one(group, half, k):
        if half == 0:
            return V.at[group, half, y, (x + k + SIDE) % SIDE]
        return V.at[group, half, (y + k + SIDE) % SIDE, x]

    def line(group, half, k):
        if half == 0:
            return V.at[group, half, (y + k + SIDE) % SIDE]
        return V.at[group, half, :, (x + k + SIDE) % SIDE]

    own_copies = [
        pltpu.make_async_copy(own_block(g, h), one(g, h, 0), local_sem.at[2 * g + h])
        for g in range(4) for h in range(2)
    ]
    c_copy = pltpu.make_async_copy(c_ref, C_in, local_sem.at[8])
    for copy in own_copies:
        copy.start()
    c_copy.start()

    def ring_stage(base, own, slot, device, split):
        first, second = pl.ds(0, split), pl.ds(split, split)
        return (
            remote(own, slot(0), ring, base, device(1)),
            remote(own, slot(0), ring, base + 1, device(-1)),
            remote(slot(-1).at[first], slot(-1).at[first], ring, base + 2, device(1)),
            remote(slot(1).at[second], slot(1).at[second], ring, base + 3, device(-1)),
        )

    def begin(stage):
        stage[0].start()
        stage[1].start()

    def pass_on(stage):
        stage[0].wait_recv()
        stage[2].start()
        stage[1].wait_recv()
        stage[3].start()

    def finish(stage):
        stage[2].wait_recv()
        stage[3].wait_recv()

    near, far = {}, {}
    for g in range(4):
        for h in range(2):
            base = 8 * (2 * g + h)
            axes = (at_x, at_y) if h == 0 else (at_y, at_x)
            near[g, h] = [
                remote(own_block(g, h), one(g, h, 0), ring, base + i, axes[0](k))
                for i, k in enumerate((1, -1, 2))
            ]
            far[g, h] = ring_stage(
                base + 4, line(g, h, 0), lambda k, g=g, h=h: line(g, h, k), axes[1], 2
            )

    def near_to_far(g):
        for h in range(2):
            for copy in near[g, h]:
                copy.wait_recv()
            begin(far[g, h])

    def far_pass(g):
        for h in range(2):
            pass_on(far[g, h])

    def far_finish(g):
        for h in range(2):
            finish(far[g, h])

    ends = (row + last) // (last + 1) + (2 * last - row) // (last + 1)
    from_lower = ((GROUP - 1 - rank) // (GROUP - 1)) * ((group_at + groups - 1) // groups)
    from_upper = ((GROUP - 1 - rank) // (GROUP - 1)) * ((2 * (groups - 1) - group_at) // groups)
    pl.semaphore_wait(barrier, 6 + ends + from_lower + from_upper)
    for g in range(4):
        for h in range(2):
            for copy in near[g, h]:
                copy.start()

    for s in range(2):
        gram_in[s, :HALF, HALF:] = jnp.zeros((HALF, HALF), jnp.float32)
        t_u[s, :HALF, HALF:] = jnp.zeros((HALF, HALF), jnp.float32)

    @pl.when(row == last)
    def _():
        for s in range(2):
            gram_in[s, HALF:] = jnp.zeros((HALF, NB), jnp.float32)
            gram_in[s, :HALF, :HALF] = jnp.zeros((HALF, HALF), jnp.float32)

    @pl.when(group_at == groups - 1)
    def _():
        Z[...] = jnp.zeros_like(Z)

    @pl.when(row == 0)
    def _():
        p_in[...] = jnp.zeros_like(p_in)

    for copy in own_copies:
        copy.wait()
    near_to_far(0)
    near_to_far(1)
    c_copy.wait()
    Ct[...] = C_in[...].T
    far_pass(0)
    near_to_far(2)
    far_pass(1)
    near_to_far(3)

    def x_up(s):
        return V[0, s].reshape(NB, NB)

    def x_low(s):
        return V[3, s].reshape(NB, NB)

    def a_up(s):
        return V[1 + s, 1].reshape(NB, NB)

    def a_low(s):
        return V[1 + s, 0].reshape(NB, NB)

    def triangle(source, target, s, base, device):
        return [
            remote(
                source.at[s, pl.ds(0, HALF), pl.ds(0, HALF)], target.at[s, pl.ds(0, HALF), pl.ds(0, HALF)],
                rows, base, device,
            ),
            remote(
                source.at[s, pl.ds(HALF, HALF)], target.at[s, pl.ds(HALF, HALF)], rows, base + 1, device
            ),
        ]

    gram_up = [triangle(gram_u, gram_in, s, 2 * s, above) for s in range(2)]
    t_down = [triangle(t_l, t_u, s, 4 + 2 * s, below) for s in range(2)]
    p_down = [remote(p_own.at[s], p_in.at[s], rows, 8 + s, below) for s in range(2)]
    pieces = [pl.ds(k * PIECE, PIECE) for k in range(PIECES)]
    q_up = [
        [
            remote(q_own.at[s, piece], q_in.at[s, piece], chain, s * PIECES + k, above)
            for k, piece in enumerate(pieces)
        ]
        for s in range(2)
    ]
    n_up = [remote(n_own.at[s], n_in.at[s], rows, 10 + s, above) for s in range(2)]

    def jump(s, k, distance):
        return pltpu.make_async_remote_copy(
            src_ref=P_own.at[s, pieces[k]], dst_ref=Z.at[s, pieces[k]],
            send_sem=jump_send.at[(s * PIECES + k) * GROUP + distance - 1],
            recv_sem=jump_recv.at[s * PIECES + k],
            device_id=up(distance), device_id_type=MESH,
        )

    def hand_on(s, k):
        return pltpu.make_async_remote_copy(
            src_ref=Z.at[s, pieces[k]], dst_ref=Z.at[s, pieces[k]],
            send_sem=jump_send.at[(s * PIECES + k) * GROUP + 1],
            recv_sem=jump_recv.at[s * PIECES + k],
            device_id=partner, device_id_type=MESH,
        )

    def compose_top(s):
        @pl.when(has_source & is_top)
        def _():
            n_own[s] = m_t[s]
            n_up[s].start()

    def compose_rest(s, takes):
        @pl.when(has_source & takes)
        def _():
            n_up[s].wait_recv()
            n_own[s] = mm(n_in[s], m_t[s])

        @pl.when(has_source & takes & (rank > 0))
        def _():
            n_up[s].start()

    def upper_gram(s):
        gram_u[s] = mmt(x_up(s), x_up(s))

        @pl.when(has_above)
        def _():
            for copy in gram_up[s]:
                copy.start()

    far_finish(0)
    for s in range(2):
        upper_gram(s)
    far_pass(2)
    far_finish(1)
    gram_a[0] = mmt(a_up(0), a_up(0)) + mmt(a_low(0), a_low(0))
    far_pass(3)
    far_finish(2)
    gram_a[1] = mmt(a_up(1), a_up(1)) + mmt(a_low(1), a_low(1))
    pair = lower_inverses([gram_a[0], gram_a[1]])
    for s in range(2):
        t_a[s] = pair[s]
        b_2[s] = mm(t_a[s], mmt(a_up(s), x_up(s)))

    def local_part(s):
        upper, lower = Ct[:, :NB], Ct[:, NB:]
        w_own[...] = mmt(upper, a_up(s)) + mmt(lower, a_low(s))
        q_own[s] = mmt(upper, x_up(s)) - mm(w_own[...], b_2[s])

    local_part(0)
    far_finish(3)
    gram_l[0] = mmt(x_low(0), x_low(0))

    gram_l[1] = mmt(x_low(1), x_low(1))
    p_own[0] = mmt(Ct[:, NB:], x_low(0))

    @pl.when(has_below)
    def _():
        p_down[0].start()
        for s in range(2):
            for copy in gram_up[s]:
                copy.wait_recv()

    for s in range(2):
        g_t[s] = mmt(x_low(s), a_low(s))
    pair = lower_inverses([gram_l[0] + gram_in[0], gram_l[1] + gram_in[1]])
    for s in range(2):
        t_l[s] = pair[s]

    @pl.when(has_below)
    def _():
        for copy in t_down[0] + t_down[1]:
            copy.start()

    for s in range(2):
        b_1[s] = mm(t_l[s], g_t[s])
        m_t[s] = mm(b_1[s], b_2[s])

    @pl.when(row == 0)
    def _():
        own = lower_inverses([gram_u[0], gram_u[1]])
        for s in range(2):
            t_u[s] = own[s]

    def receive(s, k, takes, hands):
        @pl.when(takes)
        def _():
            jump(s, k, GROUP).wait_recv()

        @pl.when(hands)
        def _():
            hand_on(s, k).start()

    q_own[0] += mm(p_own[0], m_t[0])
    for s in range(2):
        if s == 1:
            for k in range(PIECES):
                receive(s, k, has_source & is_bottom, has_source & is_bottom)
        for k, piece in enumerate(pieces):

            @pl.when(rank < GROUP - 1)
            def _():
                q_up[s][k].wait_recv()
                q_own[s, piece] += mm(q_in[s, piece], m_t[s])

            @pl.when(rank > 0)
            def _():
                q_up[s][k].start()

        if s == 0:
            compose_top(0)
            compose_top(1)
            compose_rest(0, rank < GROUP - 1)
            compose_rest(1, (rank < GROUP - 1) & (rank > 0))
        else:
            compose_rest(1, is_bottom)

        for k, piece in enumerate(pieces):

            if s == 0:
                receive(s, k, has_source, hands_on)
            else:
                receive(s, k, has_source & (rank > 0), has_source & is_top)

            @pl.when(has_source)
            def _():
                P_own[s, piece] = q_own[s, piece] + mm(Z[s, piece], n_own[s])

            @pl.when(group_at == groups - 1)
            def _():
                P_own[s, piece] = q_own[s, piece]

            @pl.when(sends_jump & (group_at > 1))
            def _():
                jump(s, k, GROUP).start()

            @pl.when(sends_jump & (group_at == 1))
            def _():
                jump(s, k, 1).start()

        @pl.when(sends_jump & (group_at > 1))
        def _():
            for k in range(PIECES):
                jump(s, k, 1).start()

        @pl.when(sends_jump & (group_at == 1))
        def _():
            for k in range(PIECES):
                jump(s, k, GROUP).start()

        @pl.when(is_top)
        def _():
            total[...] = p_own[s] + Z[s]

        @pl.when((rank < GROUP - 1) & has_source)
        def _():
            total[...] = p_own[s] + q_in[s] + mm(Z[s], n_in[s])

        @pl.when((rank < GROUP - 1) & (group_at == groups - 1))
        def _():
            total[...] = p_own[s] + q_in[s]

        if s == 0:

            @pl.when(has_above)
            def _():
                for copy in t_down[0] + [p_down[0]]:
                    copy.wait_recv()

        both = total[...]
        coeffs_a = mm(w_own[...] - mm(both, b_1[s]), t_a[s])
        coeffs_l = mm(both, t_l[s])
        upper, lower = Ct[:, :NB], Ct[:, NB:]
        lower = lower - mm(coeffs_l, x_low(s)) - mm(coeffs_a, a_low(s))
        upper = upper - mm(coeffs_a, a_up(s))
        if s == 1:

            @pl.when(has_above)
            def _():
                for copy in t_down[1] + [p_down[1]]:
                    copy.wait_recv()

        upper = upper - mm(mm(p_in[s] + P_own[s], t_u[s]), x_up(s))
        Ct[:, NB:] = lower
        Ct[:, :NB] = upper
        if s == 0:
            p_own[1] = mmt(lower, x_low(1))
            local_part(1)
            q_own[1] += mm(p_own[1], m_t[1])

            @pl.when(has_below)
            def _():
                p_down[1].start()

    o_ref[...] = Ct[...].T

    for stages in (near, far):
        for stage in stages.values():
            for copy in stage:
                copy.wait_send()

    @pl.when(has_above)
    def _():
        for copy in gram_up[0] + gram_up[1]:
            copy.wait_send()

    @pl.when(rank > 0)
    def _():
        for copy in q_up[0] + q_up[1]:
            copy.wait_send()

    @pl.when(has_source & (rank > 0))
    def _():
        for copy in n_up:
            copy.wait_send()

    @pl.when(sends_jump)
    def _():
        for s in range(2):
            for k in range(PIECES):
                jump(s, k, 1).wait_send()
                jump(s, k, GROUP).wait_send()

    @pl.when(hands_on)
    def _():
        for s in range(2):
            for k in range(PIECES):
                hand_on(s, k).wait_send()

    @pl.when(has_below)
    def _():
        for copy in t_down[0] + t_down[1] + p_down:
            copy.wait_send()


def on_device(eigenvectors, aligned_vectors, straddle_vectors):
    columns = eigenvectors.shape[1]
    in_place = pl.BlockSpec(memory_space=pltpu.HBM)
    square = pltpu.VMEM((2, NB, NB), jnp.float32)
    product = pltpu.VMEM((2, columns, NB), jnp.float32)
    dma = pltpu.SemaphoreType.DMA
    return pl.pallas_call(
        kernel,
        out_shape=jax.ShapeDtypeStruct(eigenvectors.shape, jnp.float32),
        in_specs=[in_place] * 3,
        out_specs=pl.BlockSpec(memory_space=pltpu.VMEM),
        scratch_shapes=[
            pltpu.VMEM((4, 2, SIDE, SIDE, NB // SIDE**2, NB), jnp.float32),
            pltpu.VMEM(eigenvectors.shape, jnp.float32),
            pltpu.VMEM((columns, SPAN), jnp.float32),
        ]
        + [square] * 13
        + [product] * 6
        + [pltpu.VMEM((columns, NB), jnp.float32)] * 2
        + [dma((64,)), dma((64,)), dma((12,)), dma((12,))]
        + [dma((2 * PIECES,)), dma((2 * PIECES,))]
        + [dma((2 * PIECES * GROUP,)), dma((2 * PIECES,)), dma((9,))],
        compiler_params=pltpu.CompilerParams(
            collective_id=0, has_side_effects=True, vmem_limit_bytes=40 * 1024 * 1024
        ),
    )(
        pltpu.with_memory_space_constraint(eigenvectors, pltpu.HBM),
        pltpu.with_memory_space_constraint(jnp.swapaxes(aligned_vectors, 1, 2), pltpu.HBM),
        pltpu.with_memory_space_constraint(jnp.swapaxes(straddle_vectors, 1, 2), pltpu.HBM),
    )


def solution(mesh):
    placed = (P("row", "col"), P(None, "row", "col"), P(None, "row", "col"))
    return jax.shard_map(
        on_device, mesh=mesh, in_specs=placed, out_specs=P("row", "col"), check_vma=False
    )
```

```python
import jax
import jax.numpy as jnp
from jax import lax
from jax.experimental import pallas as pl
from jax.experimental.pallas import tpu as pltpu
from jax.sharding import PartitionSpec as P

NB = 256
SPAN = 2 * NB
HALF = NB // 2
SIDE = 4
PIECES = 8
PIECE = 128 // PIECES
MESH = pl.DeviceIdType.MESH
HIGH = lax.Precision.HIGH


def mm(left, right):
    return lax.dot_general(
        left, right, (((1,), (0,)), ((), ())), precision=HIGH, preferred_element_type=jnp.float32
    )


def mmt(left, right):
    return lax.dot_general(
        left, right, (((1,), (1,)), ((), ())), precision=HIGH, preferred_element_type=jnp.float32
    )


def lower_inverses(grams):
    row = lax.broadcasted_iota(jnp.int32, (NB, NB), 0)
    col = lax.broadcasted_iota(jnp.int32, (NB, NB), 1)
    on_diagonal = row == col
    eye = jnp.where(on_diagonal, 1.0, 0.0)
    small = (row // 32 == col // 32) & (row > col)
    down = [0.5 * jnp.sum(jnp.where(on_diagonal, g, 0.0), axis=1, keepdims=True) for g in grams]
    across = [0.5 * jnp.sum(jnp.where(on_diagonal, g, 0.0), axis=0, keepdims=True) for g in grams]
    powers = [jnp.where(small, g, 0.0) / d for g, d in zip(grams, down)]
    result = [eye - n for n in powers]
    for _ in range(4):
        powers = [mm(n, n) for n in powers]
        result = [t + mm(t, n) for t, n in zip(result, powers)]
    result = [t / d for t, d in zip(result, across)]
    for size in (32, 64, 128):
        below = (row // (2 * size) == col // (2 * size)) & (row // size > col // size)
        left = [mm(t, jnp.where(below, g, 0.0)) for t, g in zip(result, grams)]
        result = [t - mm(half, t) for t, half in zip(result, left)]
    return result


def kernel(
    c_ref, a_ref, x_ref, o_ref,
    V, C_in, Ct, gram_a, gram_l, gram_u, gram_in, t_a, t_l, t_u, g_t, b_1, b_2, m_t,
    p_own, p_in, P_own, P_in, w_own,
    ring_send, ring_recv, row_send, row_recv, chain_send, chain_recv, local_sem,
):
    row = lax.axis_index("row")
    col = lax.axis_index("col")
    last = lax.axis_size("row") - 1
    y, x = col // SIDE, col % SIDE

    def at_x(step):
        return (row, y * SIDE + (x + step + SIDE) % SIDE)

    def at_y(step):
        return (row, ((y + step + SIDE) % SIDE) * SIDE + x)

    above = ((row + last) % (last + 1), col)
    below = ((row + 1) % (last + 1), col)
    has_above = row > 0
    has_below = row < last

    def remote(src, dst, sems, index, device):
        send, recv = sems
        return pltpu.make_async_remote_copy(
            src_ref=src, dst_ref=dst, send_sem=send.at[index], recv_sem=recv.at[index],
            device_id=device, device_id_type=MESH,
        )

    ring = (ring_send, ring_recv)
    rows = (row_send, row_recv)
    chain = (chain_send, chain_recv)

    barrier = pltpu.get_barrier_semaphore()
    for device in (at_x(1), at_x(2), at_x(3), at_y(1), at_y(2), at_y(3)):
        pl.semaphore_signal(barrier, inc=1, device_id=device, device_id_type=MESH)

    @pl.when(has_above)
    def _():
        pl.semaphore_signal(barrier, inc=1, device_id=above, device_id_type=MESH)

    @pl.when(has_below)
    def _():
        pl.semaphore_signal(barrier, inc=1, device_id=below, device_id_type=MESH)

    def own_block(group, half):
        upper, lower = pl.ds(0, NB), pl.ds(NB, NB)
        if group == 0:
            return x_ref.at[half, :, upper]
        if group == 3:
            return x_ref.at[half, :, lower]
        return a_ref.at[group - 1, :, upper if half == 1 else lower]

    def one(group, half, k):
        if half == 0:
            return V.at[group, half, y, (x + k + SIDE) % SIDE]
        return V.at[group, half, (y + k + SIDE) % SIDE, x]

    def line(group, half, k):
        if half == 0:
            return V.at[group, half, (y + k + SIDE) % SIDE]
        return V.at[group, half, :, (x + k + SIDE) % SIDE]

    own_copies = [
        pltpu.make_async_copy(own_block(g, h), one(g, h, 0), local_sem.at[2 * g + h])
        for g in range(4) for h in range(2)
    ]
    c_copy = pltpu.make_async_copy(c_ref, C_in, local_sem.at[8])
    for copy in own_copies:
        copy.start()
    c_copy.start()

    def ring_stage(base, own, slot, device, split):
        first, second = pl.ds(0, split), pl.ds(split, split)
        return (
            remote(own, slot(0), ring, base, device(1)),
            remote(own, slot(0), ring, base + 1, device(-1)),
            remote(slot(-1).at[first], slot(-1).at[first], ring, base + 2, device(1)),
            remote(slot(1).at[second], slot(1).at[second], ring, base + 3, device(-1)),
        )

    def begin(stage):
        stage[0].start()
        stage[1].start()

    def pass_on(stage):
        stage[0].wait_recv()
        stage[2].start()
        stage[1].wait_recv()
        stage[3].start()

    def finish(stage):
        stage[2].wait_recv()
        stage[3].wait_recv()

    near, far = {}, {}
    for g in range(4):
        for h in range(2):
            base = 8 * (2 * g + h)
            axes = (at_x, at_y) if h == 0 else (at_y, at_x)
            near[g, h] = [
                remote(own_block(g, h), one(g, h, 0), ring, base + i, axes[0](k))
                for i, k in enumerate((1, -1, 2))
            ]
            far[g, h] = ring_stage(
                base + 4, line(g, h, 0), lambda k, g=g, h=h: line(g, h, k), axes[1], 2
            )

    def near_to_far(g):
        for h in range(2):
            for copy in near[g, h]:
                copy.wait_recv()
            begin(far[g, h])

    def far_pass(g):
        for h in range(2):
            pass_on(far[g, h])

    def far_finish(g):
        for h in range(2):
            finish(far[g, h])

    ends = (row + last) // (last + 1) + (2 * last - row) // (last + 1)
    pl.semaphore_wait(barrier, 6 + ends)
    for g in range(4):
        for h in range(2):
            for copy in near[g, h]:
                copy.start()

    for s in range(2):
        gram_in[s, :HALF, HALF:] = jnp.zeros((HALF, HALF), jnp.float32)
        t_u[s, :HALF, HALF:] = jnp.zeros((HALF, HALF), jnp.float32)

    @pl.when(row == last)
    def _():
        for s in range(2):
            gram_in[s, HALF:] = jnp.zeros((HALF, NB), jnp.float32)
            gram_in[s, :HALF, :HALF] = jnp.zeros((HALF, HALF), jnp.float32)
        P_in[...] = jnp.zeros_like(P_in)

    @pl.when(row == 0)
    def _():
        p_in[...] = jnp.zeros_like(p_in)

    for copy in own_copies:
        copy.wait()
    near_to_far(0)
    near_to_far(1)
    c_copy.wait()
    Ct[...] = C_in[...].T
    far_pass(0)
    near_to_far(2)
    far_pass(1)
    near_to_far(3)

    def x_up(s):
        return V[0, s].reshape(NB, NB)

    def x_low(s):
        return V[3, s].reshape(NB, NB)

    def a_up(s):
        return V[1 + s, 1].reshape(NB, NB)

    def a_low(s):
        return V[1 + s, 0].reshape(NB, NB)

    def triangle(source, target, s, base, device):
        return [
            remote(
                source.at[s, pl.ds(0, HALF), pl.ds(0, HALF)], target.at[s, pl.ds(0, HALF), pl.ds(0, HALF)],
                rows, base, device,
            ),
            remote(
                source.at[s, pl.ds(HALF, HALF)], target.at[s, pl.ds(HALF, HALF)], rows, base + 1, device
            ),
        ]

    gram_up = [triangle(gram_u, gram_in, s, 2 * s, above) for s in range(2)]
    t_down = [triangle(t_l, t_u, s, 4 + 2 * s, below) for s in range(2)]
    p_down = [remote(p_own.at[s], p_in.at[s], rows, 8 + s, below) for s in range(2)]
    def P_up(s, k):
        piece = pl.ds(pl.multiple_of(k * PIECE, PIECE), PIECE)
        return remote(P_own.at[s, piece], P_in.at[s, piece], chain, s * PIECES + k, above)

    def upper_gram(s):
        gram_u[s] = mmt(x_up(s), x_up(s))

        @pl.when(has_above)
        def _():
            for copy in gram_up[s]:
                copy.start()

    far_finish(0)
    for s in range(2):
        upper_gram(s)
    far_pass(2)
    far_finish(1)
    gram_a[0] = mmt(a_up(0), a_up(0)) + mmt(a_low(0), a_low(0))
    far_pass(3)
    far_finish(2)
    gram_a[1] = mmt(a_up(1), a_up(1)) + mmt(a_low(1), a_low(1))
    pair = lower_inverses([gram_a[0], gram_a[1]])
    for s in range(2):
        t_a[s] = pair[s]
        b_2[s] = mm(t_a[s], mmt(a_up(s), x_up(s)))

    def local_part(s):
        upper, lower = Ct[:, :NB], Ct[:, NB:]
        w_own[...] = mmt(upper, a_up(s)) + mmt(lower, a_low(s))
        P_own[s] = mmt(upper, x_up(s)) - mm(w_own[...], b_2[s])

    local_part(0)
    far_finish(3)
    gram_l[0] = mmt(x_low(0), x_low(0))

    gram_l[1] = mmt(x_low(1), x_low(1))
    p_own[0] = mmt(Ct[:, NB:], x_low(0))

    @pl.when(has_below)
    def _():
        p_down[0].start()
        for s in range(2):
            for copy in gram_up[s]:
                copy.wait_recv()

    for s in range(2):
        g_t[s] = mmt(x_low(s), a_low(s))
    pair = lower_inverses([gram_l[0] + gram_in[0], gram_l[1] + gram_in[1]])
    for s in range(2):
        t_l[s] = pair[s]

    @pl.when(has_below)
    def _():
        for copy in t_down[0] + t_down[1]:
            copy.start()

    for s in range(2):
        b_1[s] = mm(t_l[s], g_t[s])
        m_t[s] = mm(b_1[s], b_2[s])

    @pl.when(row == 0)
    def _():
        own = lower_inverses([gram_u[0], gram_u[1]])
        for s in range(2):
            t_u[s] = own[s]

    def drain():
        for stages in (near, far):
            for stage in stages.values():
                for copy in stage:
                    copy.wait_send()

    P_own[0] += mm(p_own[0], m_t[0])

    @pl.when(row < last - 1)
    def _():
        drain()

    for s in range(2):
        @pl.loop(0, PIECES)
        def _(k):
            piece = pl.ds(pl.multiple_of(k * PIECE, PIECE), PIECE)

            @pl.when(has_below)
            def _():
                P_up(s, k).wait_recv()
                P_own[s, piece] += mm(P_in[s, piece], m_t[s])

            @pl.when(has_above)
            def _():
                P_up(s, k).start()

        if s == 0:

            @pl.when(has_above)
            def _():
                for copy in t_down[0] + [p_down[0]]:
                    copy.wait_recv()

        both = p_own[s] + P_in[s]
        coeffs_a = mm(w_own[...] - mm(both, b_1[s]), t_a[s])
        coeffs_l = mm(both, t_l[s])
        upper, lower = Ct[:, :NB], Ct[:, NB:]
        lower = lower - mm(coeffs_l, x_low(s)) - mm(coeffs_a, a_low(s))
        upper = upper - mm(coeffs_a, a_up(s))
        if s == 1:

            @pl.when(has_above)
            def _():
                for copy in t_down[1] + [p_down[1]]:
                    copy.wait_recv()

        upper = upper - mm(mm(p_in[s] + P_own[s], t_u[s]), x_up(s))
        Ct[:, NB:] = lower
        Ct[:, :NB] = upper
        if s == 0:
            p_own[1] = mmt(lower, x_low(1))
            local_part(1)
            P_own[1] += mm(p_own[1], m_t[1])

            @pl.when(has_below)
            def _():
                p_down[1].start()

    o_ref[...] = Ct[...].T

    @pl.when(row >= last - 1)
    def _():
        drain()

    @pl.when(has_above)
    def _():
        for copy in gram_up[0] + gram_up[1]:
            copy.wait_send()

        @pl.loop(0, PIECES)
        def _(k):
            for s in range(2):
                P_up(s, k).wait_send()

    @pl.when(has_below)
    def _():
        for copy in t_down[0] + t_down[1] + p_down:
            copy.wait_send()


def on_device(eigenvectors, aligned_vectors, straddle_vectors):
    columns = eigenvectors.shape[1]
    in_place = pl.BlockSpec(memory_space=pltpu.HBM)
    square = pltpu.VMEM((2, NB, NB), jnp.float32)
    product = pltpu.VMEM((2, columns, NB), jnp.float32)
    dma = pltpu.SemaphoreType.DMA
    return pl.pallas_call(
        kernel,
        out_shape=jax.ShapeDtypeStruct(eigenvectors.shape, jnp.float32),
        in_specs=[in_place] * 3,
        out_specs=pl.BlockSpec(memory_space=pltpu.VMEM),
        scratch_shapes=[
            pltpu.VMEM((4, 2, SIDE, SIDE, NB // SIDE**2, NB), jnp.float32),
            pltpu.VMEM(eigenvectors.shape, jnp.float32),
            pltpu.VMEM((columns, SPAN), jnp.float32),
        ]
        + [square] * 11
        + [product] * 4
        + [pltpu.VMEM((columns, NB), jnp.float32)]
        + [dma((64,)), dma((64,)), dma((10,)), dma((10,)), dma((2 * PIECES,)), dma((2 * PIECES,)), dma((9,))],
        compiler_params=pltpu.CompilerParams(
            collective_id=0, has_side_effects=True, vmem_limit_bytes=40 * 1024 * 1024
        ),
    )(
        pltpu.with_memory_space_constraint(eigenvectors, pltpu.HBM),
        pltpu.with_memory_space_constraint(jnp.swapaxes(aligned_vectors, 1, 2), pltpu.HBM),
        pltpu.with_memory_space_constraint(jnp.swapaxes(straddle_vectors, 1, 2), pltpu.HBM),
    )


def solution(mesh):
    placed = (P("row", "col"), P(None, "row", "col"), P(None, "row", "col"))
    return jax.shard_map(
        on_device, mesh=mesh, in_specs=placed, out_specs=P("row", "col"), check_vma=False
    )
```

```python
import jax
import jax.numpy as jnp
from jax import lax
from jax.experimental import pallas as pl
from jax.experimental.pallas import tpu as pltpu
from jax.sharding import PartitionSpec as P

NB = 256
SPAN = 2 * NB
HALF = NB // 2
SIDE = 4
PIECES = 8
PIECE = 128 // PIECES
MESH = pl.DeviceIdType.MESH
HIGH = lax.Precision.HIGH


def mm(left, right):
    return lax.dot_general(
        left, right, (((1,), (0,)), ((), ())), precision=HIGH, preferred_element_type=jnp.float32
    )


def mmt(left, right):
    return lax.dot_general(
        left, right, (((1,), (1,)), ((), ())), precision=HIGH, preferred_element_type=jnp.float32
    )


def lower_inverses(grams):
    row = lax.broadcasted_iota(jnp.int32, (NB, NB), 0)
    col = lax.broadcasted_iota(jnp.int32, (NB, NB), 1)
    on_diagonal = row == col
    eye = jnp.where(on_diagonal, 1.0, 0.0)
    small = (row // 32 == col // 32) & (row > col)
    down = [0.5 * jnp.sum(jnp.where(on_diagonal, g, 0.0), axis=1, keepdims=True) for g in grams]
    across = [0.5 * jnp.sum(jnp.where(on_diagonal, g, 0.0), axis=0, keepdims=True) for g in grams]
    powers = [jnp.where(small, g, 0.0) / d for g, d in zip(grams, down)]
    result = [eye - n for n in powers]
    for _ in range(4):
        powers = [mm(n, n) for n in powers]
        result = [t + mm(t, n) for t, n in zip(result, powers)]
    result = [t / d for t, d in zip(result, across)]
    for size in (32, 64, 128):
        below = (row // (2 * size) == col // (2 * size)) & (row // size > col // size)
        left = [mm(t, jnp.where(below, g, 0.0)) for t, g in zip(result, grams)]
        result = [t - mm(half, t) for t, half in zip(result, left)]
    return result


def kernel(
    c_ref, a_ref, x_ref, o_ref,
    V, C_in, Ct, gram_a, gram_l, gram_u, gram_in, t_a, t_l, t_u, g_t, b_1, b_2, m_t,
    p_own, p_in, P_own, P_in, w_own,
    ring_send, ring_recv, row_send, row_recv, chain_send, chain_recv, local_sem,
):
    row = lax.axis_index("row")
    col = lax.axis_index("col")
    last = lax.axis_size("row") - 1
    y, x = col // SIDE, col % SIDE

    def at_x(step):
        return (row, y * SIDE + (x + step + SIDE) % SIDE)

    def at_y(step):
        return (row, ((y + step + SIDE) % SIDE) * SIDE + x)

    above = ((row + last) % (last + 1), col)
    below = ((row + 1) % (last + 1), col)
    has_above = row > 0
    has_below = row < last

    def remote(src, dst, sems, index, device):
        send, recv = sems
        return pltpu.make_async_remote_copy(
            src_ref=src, dst_ref=dst, send_sem=send.at[index], recv_sem=recv.at[index],
            device_id=device, device_id_type=MESH,
        )

    ring = (ring_send, ring_recv)
    rows = (row_send, row_recv)
    chain = (chain_send, chain_recv)

    barrier = pltpu.get_barrier_semaphore()
    for device in (at_x(1), at_x(2), at_x(3), at_y(1), at_y(2), at_y(3)):
        pl.semaphore_signal(barrier, inc=1, device_id=device, device_id_type=MESH)

    @pl.when(has_above)
    def _():
        pl.semaphore_signal(barrier, inc=1, device_id=above, device_id_type=MESH)

    @pl.when(has_below)
    def _():
        pl.semaphore_signal(barrier, inc=1, device_id=below, device_id_type=MESH)

    def own_block(group, half):
        upper, lower = pl.ds(0, NB), pl.ds(NB, NB)
        if group == 0:
            return x_ref.at[half, :, upper]
        if group == 3:
            return x_ref.at[half, :, lower]
        return a_ref.at[group - 1, :, upper if half == 1 else lower]

    def one(group, half, k):
        if half == 0:
            return V.at[group, half, y, (x + k + SIDE) % SIDE]
        return V.at[group, half, (y + k + SIDE) % SIDE, x]

    def line(group, half, k):
        if half == 0:
            return V.at[group, half, (y + k + SIDE) % SIDE]
        return V.at[group, half, :, (x + k + SIDE) % SIDE]

    own_copies = [
        pltpu.make_async_copy(own_block(g, h), one(g, h, 0), local_sem.at[2 * g + h])
        for g in range(4) for h in range(2)
    ]
    c_copy = pltpu.make_async_copy(c_ref, C_in, local_sem.at[8])
    for copy in own_copies:
        copy.start()
    c_copy.start()

    def ring_stage(base, own, slot, device, split):
        first, second = pl.ds(0, split), pl.ds(split, split)
        return (
            remote(own, slot(0), ring, base, device(1)),
            remote(own, slot(0), ring, base + 1, device(-1)),
            remote(slot(-1).at[first], slot(-1).at[first], ring, base + 2, device(1)),
            remote(slot(1).at[second], slot(1).at[second], ring, base + 3, device(-1)),
        )

    def begin(stage):
        stage[0].start()
        stage[1].start()

    def pass_on(stage):
        stage[0].wait_recv()
        stage[2].start()
        stage[1].wait_recv()
        stage[3].start()

    def finish(stage):
        stage[2].wait_recv()
        stage[3].wait_recv()

    near, far = {}, {}
    for g in range(4):
        for h in range(2):
            base = 8 * (2 * g + h)
            axes = (at_x, at_y) if h == 0 else (at_y, at_x)
            near[g, h] = [
                remote(one(g, h, 0), one(g, h, 0), ring, base + i, axes[0](k))
                for i, k in enumerate((1, -1, 2))
            ]
            far[g, h] = ring_stage(
                base + 4, line(g, h, 0), lambda k, g=g, h=h: line(g, h, k), axes[1], 2
            )

    def near_to_far(g):
        for h in range(2):
            for copy in near[g, h]:
                copy.wait_recv()
            begin(far[g, h])

    def far_pass(g):
        for h in range(2):
            pass_on(far[g, h])

    def far_finish(g):
        for h in range(2):
            finish(far[g, h])

    for copy in own_copies:
        copy.wait()
    ends = (row + last) // (last + 1) + (2 * last - row) // (last + 1)
    pl.semaphore_wait(barrier, 6 + ends)
    for g in range(4):
        for h in range(2):
            for copy in near[g, h]:
                copy.start()

    for s in range(2):
        gram_in[s, :HALF, HALF:] = jnp.zeros((HALF, HALF), jnp.float32)
        t_u[s, :HALF, HALF:] = jnp.zeros((HALF, HALF), jnp.float32)

    @pl.when(row == last)
    def _():
        for s in range(2):
            gram_in[s, HALF:] = jnp.zeros((HALF, NB), jnp.float32)
            gram_in[s, :HALF, :HALF] = jnp.zeros((HALF, HALF), jnp.float32)
        P_in[...] = jnp.zeros_like(P_in)

    @pl.when(row == 0)
    def _():
        p_in[...] = jnp.zeros_like(p_in)

    near_to_far(0)
    near_to_far(1)
    c_copy.wait()
    Ct[...] = C_in[...].T
    far_pass(0)
    near_to_far(2)
    far_pass(1)
    near_to_far(3)

    def x_up(s):
        return V[0, s].reshape(NB, NB)

    def x_low(s):
        return V[3, s].reshape(NB, NB)

    def a_up(s):
        return V[1 + s, 1].reshape(NB, NB)

    def a_low(s):
        return V[1 + s, 0].reshape(NB, NB)

    def triangle(source, target, s, base, device):
        return [
            remote(
                source.at[s, pl.ds(0, HALF), pl.ds(0, HALF)], target.at[s, pl.ds(0, HALF), pl.ds(0, HALF)],
                rows, base, device,
            ),
            remote(
                source.at[s, pl.ds(HALF, HALF)], target.at[s, pl.ds(HALF, HALF)], rows, base + 1, device
            ),
        ]

    gram_up = [triangle(gram_u, gram_in, s, 2 * s, above) for s in range(2)]
    t_down = [triangle(t_l, t_u, s, 4 + 2 * s, below) for s in range(2)]
    p_down = [remote(p_own.at[s], p_in.at[s], rows, 8 + s, below) for s in range(2)]
    def P_up(s, k):
        piece = pl.ds(pl.multiple_of(k * PIECE, PIECE), PIECE)
        return remote(P_own.at[s, piece], P_in.at[s, piece], chain, s * PIECES + k, above)

    def upper_gram(s):
        gram_u[s] = mmt(x_up(s), x_up(s))

        @pl.when(has_above)
        def _():
            for copy in gram_up[s]:
                copy.start()

    far_finish(0)
    for s in range(2):
        upper_gram(s)
    far_pass(2)
    far_finish(1)
    gram_a[0] = mmt(a_up(0), a_up(0)) + mmt(a_low(0), a_low(0))
    far_pass(3)
    far_finish(2)
    gram_a[1] = mmt(a_up(1), a_up(1)) + mmt(a_low(1), a_low(1))
    pair = lower_inverses([gram_a[0], gram_a[1]])
    for s in range(2):
        t_a[s] = pair[s]
        b_2[s] = mm(t_a[s], mmt(a_up(s), x_up(s)))

    def local_part(s):
        upper, lower = Ct[:, :NB], Ct[:, NB:]
        w_own[...] = mmt(upper, a_up(s)) + mmt(lower, a_low(s))
        P_own[s] = mmt(upper, x_up(s)) - mm(w_own[...], b_2[s])

    local_part(0)
    far_finish(3)
    gram_l[0] = mmt(x_low(0), x_low(0))

    gram_l[1] = mmt(x_low(1), x_low(1))
    p_own[0] = mmt(Ct[:, NB:], x_low(0))

    @pl.when(has_below)
    def _():
        p_down[0].start()
        for s in range(2):
            for copy in gram_up[s]:
                copy.wait_recv()

    for s in range(2):
        g_t[s] = mmt(x_low(s), a_low(s))
    pair = lower_inverses([gram_l[0] + gram_in[0], gram_l[1] + gram_in[1]])
    for s in range(2):
        t_l[s] = pair[s]

    @pl.when(has_below)
    def _():
        for copy in t_down[0] + t_down[1]:
            copy.start()

    for s in range(2):
        b_1[s] = mm(t_l[s], g_t[s])
        m_t[s] = mm(b_1[s], b_2[s])

    @pl.when(row == 0)
    def _():
        own = lower_inverses([gram_u[0], gram_u[1]])
        for s in range(2):
            t_u[s] = own[s]

    def drain():
        for stages in (near, far):
            for stage in stages.values():
                for copy in stage:
                    copy.wait_send()

    P_own[0] += mm(p_own[0], m_t[0])

    @pl.when(row < last - 1)
    def _():
        drain()

    for s in range(2):
        @pl.loop(0, PIECES)
        def _(k):
            piece = pl.ds(pl.multiple_of(k * PIECE, PIECE), PIECE)

            @pl.when(has_below)
            def _():
                P_up(s, k).wait_recv()
                P_own[s, piece] += mm(P_in[s, piece], m_t[s])

            @pl.when(has_above)
            def _():
                P_up(s, k).start()

        if s == 0:

            @pl.when(has_above)
            def _():
                for copy in t_down[0] + [p_down[0]]:
                    copy.wait_recv()

        both = p_own[s] + P_in[s]
        coeffs_a = mm(w_own[...] - mm(both, b_1[s]), t_a[s])
        coeffs_l = mm(both, t_l[s])
        upper, lower = Ct[:, :NB], Ct[:, NB:]
        lower = lower - mm(coeffs_l, x_low(s)) - mm(coeffs_a, a_low(s))
        upper = upper - mm(coeffs_a, a_up(s))
        if s == 1:

            @pl.when(has_above)
            def _():
                for copy in t_down[1] + [p_down[1]]:
                    copy.wait_recv()

        upper = upper - mm(mm(p_in[s] + P_own[s], t_u[s]), x_up(s))
        Ct[:, NB:] = lower
        Ct[:, :NB] = upper
        if s == 0:
            p_own[1] = mmt(lower, x_low(1))
            local_part(1)
            P_own[1] += mm(p_own[1], m_t[1])

            @pl.when(has_below)
            def _():
                p_down[1].start()

    o_ref[...] = Ct[...].T

    @pl.when(row >= last - 1)
    def _():
        drain()

    @pl.when(has_above)
    def _():
        for copy in gram_up[0] + gram_up[1]:
            copy.wait_send()

        @pl.loop(0, PIECES)
        def _(k):
            for s in range(2):
                P_up(s, k).wait_send()

    @pl.when(has_below)
    def _():
        for copy in t_down[0] + t_down[1] + p_down:
            copy.wait_send()


def on_device(eigenvectors, aligned_vectors, straddle_vectors):
    columns = eigenvectors.shape[1]
    in_place = pl.BlockSpec(memory_space=pltpu.HBM)
    square = pltpu.VMEM((2, NB, NB), jnp.float32)
    product = pltpu.VMEM((2, columns, NB), jnp.float32)
    dma = pltpu.SemaphoreType.DMA
    return pl.pallas_call(
        kernel,
        out_shape=jax.ShapeDtypeStruct(eigenvectors.shape, jnp.float32),
        in_specs=[in_place] * 3,
        out_specs=pl.BlockSpec(memory_space=pltpu.VMEM),
        scratch_shapes=[
            pltpu.VMEM((4, 2, SIDE, SIDE, NB // SIDE**2, NB), jnp.float32),
            pltpu.VMEM(eigenvectors.shape, jnp.float32),
            pltpu.VMEM((columns, SPAN), jnp.float32),
        ]
        + [square] * 11
        + [product] * 4
        + [pltpu.VMEM((columns, NB), jnp.float32)]
        + [dma((64,)), dma((64,)), dma((10,)), dma((10,)), dma((2 * PIECES,)), dma((2 * PIECES,)), dma((9,))],
        compiler_params=pltpu.CompilerParams(
            collective_id=0, has_side_effects=True, vmem_limit_bytes=40 * 1024 * 1024
        ),
    )(
        pltpu.with_memory_space_constraint(eigenvectors, pltpu.HBM),
        pltpu.with_memory_space_constraint(jnp.swapaxes(aligned_vectors, 1, 2), pltpu.HBM),
        pltpu.with_memory_space_constraint(jnp.swapaxes(straddle_vectors, 1, 2), pltpu.HBM),
    )


def solution(mesh):
    placed = (P("row", "col"), P(None, "row", "col"), P(None, "row", "col"))
    return jax.shard_map(
        on_device, mesh=mesh, in_specs=placed, out_specs=P("row", "col"), check_vma=False
    )
```

```python
import jax
import jax.numpy as jnp
from jax import lax
from jax.experimental import pallas as pl
from jax.experimental.pallas import tpu as pltpu
from jax.sharding import PartitionSpec as P

NB = 256
SPAN = 2 * NB
HALF = NB // 2
SIDE = 4
PIECES = 8
PIECE = 128 // PIECES
MESH = pl.DeviceIdType.MESH
HIGH = lax.Precision.HIGH


def mm(left, right):
    return lax.dot_general(
        left, right, (((1,), (0,)), ((), ())), precision=HIGH, preferred_element_type=jnp.float32
    )


def mmt(left, right):
    return lax.dot_general(
        left, right, (((1,), (1,)), ((), ())), precision=HIGH, preferred_element_type=jnp.float32
    )


def lower_inverses(grams):
    row = lax.broadcasted_iota(jnp.int32, (NB, NB), 0)
    col = lax.broadcasted_iota(jnp.int32, (NB, NB), 1)
    on_diagonal = row == col
    eye = jnp.where(on_diagonal, 1.0, 0.0)
    small = (row // 32 == col // 32) & (row > col)
    down = [0.5 * jnp.sum(jnp.where(on_diagonal, g, 0.0), axis=1, keepdims=True) for g in grams]
    across = [0.5 * jnp.sum(jnp.where(on_diagonal, g, 0.0), axis=0, keepdims=True) for g in grams]
    powers = [jnp.where(small, g, 0.0) / d for g, d in zip(grams, down)]
    result = [eye - n for n in powers]
    for _ in range(4):
        powers = [mm(n, n) for n in powers]
        result = [t + mm(t, n) for t, n in zip(result, powers)]
    result = [t / d for t, d in zip(result, across)]
    for size in (32, 64, 128):
        below = (row // (2 * size) == col // (2 * size)) & (row // size > col // size)
        left = [mm(t, jnp.where(below, g, 0.0)) for t, g in zip(result, grams)]
        result = [t - mm(half, t) for t, half in zip(result, left)]
    return result


def kernel(
    c_ref, a_ref, x_ref, o_ref,
    V, C_in, Ct, gram_a, gram_l, gram_u, gram_in, t_a, t_l, t_u, g_t, b_1, b_2, m_t,
    p_own, p_in, P_own, P_in, w_own,
    ring_send, ring_recv, row_send, row_recv, chain_send, chain_recv, local_sem,
):
    row = lax.axis_index("row")
    col = lax.axis_index("col")
    last = lax.axis_size("row") - 1
    y, x = col // SIDE, col % SIDE

    def at_x(step):
        return (row, y * SIDE + (x + step + SIDE) % SIDE)

    def at_y(step):
        return (row, ((y + step + SIDE) % SIDE) * SIDE + x)

    above = ((row + last) % (last + 1), col)
    below = ((row + 1) % (last + 1), col)
    has_above = row > 0
    has_below = row < last

    def remote(src, dst, sems, index, device):
        send, recv = sems
        return pltpu.make_async_remote_copy(
            src_ref=src, dst_ref=dst, send_sem=send.at[index], recv_sem=recv.at[index],
            device_id=device, device_id_type=MESH,
        )

    ring = (ring_send, ring_recv)
    rows = (row_send, row_recv)
    chain = (chain_send, chain_recv)

    def own_block(group, half):
        upper, lower = pl.ds(0, NB), pl.ds(NB, NB)
        if group == 0:
            return x_ref.at[half, :, upper]
        if group == 3:
            return x_ref.at[half, :, lower]
        return a_ref.at[group - 1, :, upper if half == 1 else lower]

    def one(group, half, k):
        if half == 0:
            return V.at[group, half, y, (x + k + SIDE) % SIDE]
        return V.at[group, half, (y + k + SIDE) % SIDE, x]

    def line(group, half, k):
        if half == 0:
            return V.at[group, half, (y + k + SIDE) % SIDE]
        return V.at[group, half, :, (x + k + SIDE) % SIDE]

    own_copies = [
        pltpu.make_async_copy(own_block(g, h), one(g, h, 0), local_sem.at[2 * g + h])
        for g in range(4) for h in range(2)
    ]
    c_copy = pltpu.make_async_copy(c_ref, C_in, local_sem.at[8])
    for copy in own_copies:
        copy.start()
    c_copy.start()

    barrier = pltpu.get_barrier_semaphore()
    for device in (at_x(1), at_x(2), at_x(3), at_y(1), at_y(2), at_y(3)):
        pl.semaphore_signal(barrier, inc=1, device_id=device, device_id_type=MESH)

    @pl.when(has_above)
    def _():
        pl.semaphore_signal(barrier, inc=1, device_id=above, device_id_type=MESH)

    @pl.when(has_below)
    def _():
        pl.semaphore_signal(barrier, inc=1, device_id=below, device_id_type=MESH)

    def ring_stage(base, own, slot, device, split):
        first, second = pl.ds(0, split), pl.ds(split, split)
        return (
            remote(own, slot(0), ring, base, device(1)),
            remote(own, slot(0), ring, base + 1, device(-1)),
            remote(slot(-1).at[first], slot(-1).at[first], ring, base + 2, device(1)),
            remote(slot(1).at[second], slot(1).at[second], ring, base + 3, device(-1)),
        )

    def begin(stage):
        stage[0].start()
        stage[1].start()

    def pass_on(stage):
        stage[0].wait_recv()
        stage[2].start()
        stage[1].wait_recv()
        stage[3].start()

    def finish(stage):
        stage[2].wait_recv()
        stage[3].wait_recv()

    near, far = {}, {}
    for g in range(4):
        for h in range(2):
            base = 8 * (2 * g + h)
            axes = (at_x, at_y) if h == 0 else (at_y, at_x)
            near[g, h] = [
                remote(one(g, h, 0), one(g, h, 0), ring, base + i, axes[0](k))
                for i, k in enumerate((1, -1, 2))
            ]
            far[g, h] = ring_stage(
                base + 4, line(g, h, 0), lambda k, g=g, h=h: line(g, h, k), axes[1], 2
            )

    def near_to_far(g):
        for h in range(2):
            for copy in near[g, h]:
                copy.wait_recv()
            begin(far[g, h])

    def far_pass(g):
        for h in range(2):
            pass_on(far[g, h])

    def far_finish(g):
        for h in range(2):
            finish(far[g, h])

    for copy in own_copies:
        copy.wait()
    ends = (row + last) // (last + 1) + (2 * last - row) // (last + 1)
    pl.semaphore_wait(barrier, 6 + ends)
    for g in range(4):
        for h in range(2):
            for copy in near[g, h]:
                copy.start()

    for s in range(2):
        gram_in[s, :HALF, HALF:] = jnp.zeros((HALF, HALF), jnp.float32)
        t_u[s, :HALF, HALF:] = jnp.zeros((HALF, HALF), jnp.float32)

    @pl.when(row == last)
    def _():
        for s in range(2):
            gram_in[s, HALF:] = jnp.zeros((HALF, NB), jnp.float32)
            gram_in[s, :HALF, :HALF] = jnp.zeros((HALF, HALF), jnp.float32)
        P_in[...] = jnp.zeros_like(P_in)

    @pl.when(row == 0)
    def _():
        p_in[...] = jnp.zeros_like(p_in)

    near_to_far(0)
    near_to_far(1)
    c_copy.wait()
    Ct[...] = C_in[...].T
    far_pass(0)
    near_to_far(2)
    far_pass(1)
    near_to_far(3)

    def x_up(s):
        return V[0, s].reshape(NB, NB)

    def x_low(s):
        return V[3, s].reshape(NB, NB)

    def a_up(s):
        return V[1 + s, 1].reshape(NB, NB)

    def a_low(s):
        return V[1 + s, 0].reshape(NB, NB)

    def triangle(source, target, s, base, device):
        return [
            remote(
                source.at[s, pl.ds(0, HALF), pl.ds(0, HALF)], target.at[s, pl.ds(0, HALF), pl.ds(0, HALF)],
                rows, base, device,
            ),
            remote(
                source.at[s, pl.ds(HALF, HALF)], target.at[s, pl.ds(HALF, HALF)], rows, base + 1, device
            ),
        ]

    gram_up = [triangle(gram_u, gram_in, s, 2 * s, above) for s in range(2)]
    t_down = [triangle(t_l, t_u, s, 4 + 2 * s, below) for s in range(2)]
    p_down = [remote(p_own.at[s], p_in.at[s], rows, 8 + s, below) for s in range(2)]
    def P_up(s, k):
        piece = pl.ds(pl.multiple_of(k * PIECE, PIECE), PIECE)
        return remote(P_own.at[s, piece], P_in.at[s, piece], chain, s * PIECES + k, above)

    def upper_gram(s):
        gram_u[s] = mmt(x_up(s), x_up(s))

        @pl.when(has_above)
        def _():
            for copy in gram_up[s]:
                copy.start()

    far_finish(0)
    for s in range(2):
        upper_gram(s)
    far_pass(2)
    far_finish(1)
    gram_a[0] = mmt(a_up(0), a_up(0)) + mmt(a_low(0), a_low(0))
    far_pass(3)
    far_finish(2)
    gram_a[1] = mmt(a_up(1), a_up(1)) + mmt(a_low(1), a_low(1))
    pair = lower_inverses([gram_a[0], gram_a[1]])
    for s in range(2):
        t_a[s] = pair[s]
        b_2[s] = mm(t_a[s], mmt(a_up(s), x_up(s)))

    def local_part(s):
        upper, lower = Ct[:, :NB], Ct[:, NB:]
        w_own[...] = mmt(upper, a_up(s)) + mmt(lower, a_low(s))
        P_own[s] = mmt(upper, x_up(s)) - mm(w_own[...], b_2[s])

    local_part(0)
    far_finish(3)
    gram_l[0] = mmt(x_low(0), x_low(0))

    gram_l[1] = mmt(x_low(1), x_low(1))
    p_own[0] = mmt(Ct[:, NB:], x_low(0))

    @pl.when(has_below)
    def _():
        p_down[0].start()
        for s in range(2):
            for copy in gram_up[s]:
                copy.wait_recv()

    for s in range(2):
        g_t[s] = mmt(x_low(s), a_low(s))
    pair = lower_inverses([gram_l[0] + gram_in[0], gram_l[1] + gram_in[1]])
    for s in range(2):
        t_l[s] = pair[s]

    @pl.when(has_below)
    def _():
        for copy in t_down[0] + t_down[1]:
            copy.start()

    for s in range(2):
        b_1[s] = mm(t_l[s], g_t[s])
        m_t[s] = mm(b_1[s], b_2[s])

    @pl.when(row == 0)
    def _():
        own = lower_inverses([gram_u[0], gram_u[1]])
        for s in range(2):
            t_u[s] = own[s]

    def drain():
        for stages in (near, far):
            for stage in stages.values():
                for copy in stage:
                    copy.wait_send()

    P_own[0] += mm(p_own[0], m_t[0])

    @pl.when(row < last - 1)
    def _():
        drain()

    for s in range(2):
        @pl.loop(0, PIECES)
        def _(k):
            piece = pl.ds(pl.multiple_of(k * PIECE, PIECE), PIECE)

            @pl.when(has_below)
            def _():
                P_up(s, k).wait_recv()
                P_own[s, piece] += mm(P_in[s, piece], m_t[s])

            @pl.when(has_above)
            def _():
                P_up(s, k).start()

        if s == 0:

            @pl.when(has_above)
            def _():
                for copy in t_down[0] + [p_down[0]]:
                    copy.wait_recv()

        both = p_own[s] + P_in[s]
        coeffs_a = mm(w_own[...] - mm(both, b_1[s]), t_a[s])
        coeffs_l = mm(both, t_l[s])
        upper, lower = Ct[:, :NB], Ct[:, NB:]
        lower = lower - mm(coeffs_l, x_low(s)) - mm(coeffs_a, a_low(s))
        upper = upper - mm(coeffs_a, a_up(s))
        if s == 1:

            @pl.when(has_above)
            def _():
                for copy in t_down[1] + [p_down[1]]:
                    copy.wait_recv()

        upper = upper - mm(mm(p_in[s] + P_own[s], t_u[s]), x_up(s))
        Ct[:, NB:] = lower
        Ct[:, :NB] = upper
        if s == 0:
            p_own[1] = mmt(lower, x_low(1))
            local_part(1)
            P_own[1] += mm(p_own[1], m_t[1])

            @pl.when(has_below)
            def _():
                p_down[1].start()

    o_ref[...] = Ct[...].T

    @pl.when(row >= last - 1)
    def _():
        drain()

    @pl.when(has_above)
    def _():
        for copy in gram_up[0] + gram_up[1]:
            copy.wait_send()

        @pl.loop(0, PIECES)
        def _(k):
            for s in range(2):
                P_up(s, k).wait_send()

    @pl.when(has_below)
    def _():
        for copy in t_down[0] + t_down[1] + p_down:
            copy.wait_send()


def on_device(eigenvectors, aligned_vectors, straddle_vectors):
    columns = eigenvectors.shape[1]
    in_place = pl.BlockSpec(memory_space=pltpu.HBM)
    square = pltpu.VMEM((2, NB, NB), jnp.float32)
    product = pltpu.VMEM((2, columns, NB), jnp.float32)
    dma = pltpu.SemaphoreType.DMA
    return pl.pallas_call(
        kernel,
        out_shape=jax.ShapeDtypeStruct(eigenvectors.shape, jnp.float32),
        in_specs=[in_place] * 3,
        out_specs=pl.BlockSpec(memory_space=pltpu.VMEM),
        scratch_shapes=[
            pltpu.VMEM((4, 2, SIDE, SIDE, NB // SIDE**2, NB), jnp.float32),
            pltpu.VMEM(eigenvectors.shape, jnp.float32),
            pltpu.VMEM((columns, SPAN), jnp.float32),
        ]
        + [square] * 11
        + [product] * 4
        + [pltpu.VMEM((columns, NB), jnp.float32)]
        + [dma((64,)), dma((64,)), dma((10,)), dma((10,)), dma((2 * PIECES,)), dma((2 * PIECES,)), dma((9,))],
        compiler_params=pltpu.CompilerParams(
            collective_id=0, has_side_effects=True, vmem_limit_bytes=40 * 1024 * 1024
        ),
    )(
        pltpu.with_memory_space_constraint(eigenvectors, pltpu.HBM),
        pltpu.with_memory_space_constraint(jnp.swapaxes(aligned_vectors, 1, 2), pltpu.HBM),
        pltpu.with_memory_space_constraint(jnp.swapaxes(straddle_vectors, 1, 2), pltpu.HBM),
    )


def solution(mesh):
    placed = (P("row", "col"), P(None, "row", "col"), P(None, "row", "col"))
    return jax.shard_map(
        on_device, mesh=mesh, in_specs=placed, out_specs=P("row", "col"), check_vma=False
    )
```
